32 devices in a mesh: dp: 4 (over y, core), tensor: 8 (over z, x).
Axes of the slice: x: 2, y: 2, z: 4, core: 2. Of those that a mesh axis runs over, the one named last changes fastest.
Arguments:
- block_input: float32 [4, 2048, 1024], P('dp', 'tensor'), may hold values from -6 to 6
- segment_ids: int32 [4, 2048], P('dp'), may hold values from 0 to 2, as said below
- positions: int32 [4, 2048], P('dp'), may hold values from 0 to 1791, as said below
- attention_gain: bfloat16 [1024], P('dp'), may hold values from 0.099609375 to 1.8984375
- feedforward_gain: bfloat16 [1024], P('dp'), may hold values from 0.099609375 to 1.8984375
- qkv_weight: bfloat16 [1024, 3, 1024], P('dp', None, 'tensor'), may hold values from -2 to 2, as said below
- output_weight: bfloat16 [1024, 1024], P('tensor', 'dp'), may hold values from -0.75 to 0.75
- expand_weight: bfloat16 [1024, 2, 2624], P('dp', None, 'tensor'), may hold values from -0.1875 to 0.1875
- contract_weight: bfloat16 [2624, 1024], P('tensor', 'dp'), may hold values from -0.25 to 0.25
- cotangent: float32 [4, 2048, 1024], P('dp', 'tensor'), may hold values from -6 to 6
Outputs:
- block_output: float32 [4, 2048, 1024], P('dp', 'tensor')
- input_grad: float32 [4, 2048, 1024], P('dp', 'tensor')
- attention_gain_grad: float32 [1024], P('dp')
- feedforward_gain_grad: float32 [1024], P('dp')
- qkv_grad: float32 [1024, 3, 1024], P('dp', None, 'tensor')
- output_grad: float32 [1024, 1024], P('tensor', 'dp')
- expand_grad: float32 [1024, 2, 2624], P('dp', None, 'tensor')
- contract_grad: float32 [2624, 1024], P('tensor', 'dp')
The draws below stay inside these ranges and needn't reach their ends.
Inputs may be any that keep to these rules, and one draw needn't show every extreme that they name: `segment_ids`: within each sequence the numbers never fall; a token's number tells its document, and a number may be skipped. `positions`: each token's position counts the tokens before it in its own document; no document is longer than 1792 tokens, and some document is that long. `qkv_weight`: the joined query, key and value projection.
All inputs are finite; a program needn't handle non-finite values.
Results may differ from the reference program's by a relative error of at most 0.025.
Values may be sent and summed in bfloat16 or wider, within the bound.
A program may use at most 128 MiB of HBM per device.

```python
import math
import jax
import jax.numpy as jnp
from jax import lax

D = 1024
H = 16
HD = 64
FF = 2624
WINDOW = 128
L = 2048
SEQS = 4


def document_cuts(key):
    lowest = L // 8
    first_cut = jax.random.randint(jax.random.fold_in(key, 11), (SEQS, 1), lowest, L - lowest + 1)
    second_cut = jax.random.randint(jax.random.fold_in(key, 12), (SEQS, 1), lowest, L - lowest + 1)
    leading = jnp.arange(SEQS, dtype=jnp.int32)[:, None] == 0
    first_cut = jnp.where(leading, L - lowest, first_cut).astype(jnp.int32)
    second_cut = jnp.where(leading, L - lowest, second_cut).astype(jnp.int32)
    index_row = jnp.arange(L, dtype=jnp.int32)[None, :]
    return (first_cut, second_cut, index_row)


def draw_segment_ids(key, part):
    first_cut, second_cut, index_row = document_cuts(key)
    return (index_row >= first_cut).astype(jnp.int32) + (index_row >= second_cut).astype(jnp.int32)


def draw_positions(key, part):
    first_cut, second_cut, index_row = document_cuts(key)
    begins = jnp.maximum(jnp.where(index_row >= first_cut, first_cut, 0), jnp.where(index_row >= second_cut, second_cut, 0))
    return (index_row - begins).astype(jnp.int32)


def draw_qkv_weight(key, part):
    base = jax.random.normal(jax.random.fold_in(key, 21), (D, 3, D), jnp.float32)
    return (base * D ** (-0.5)).astype(jnp.bfloat16)


def block_scale(own_key, dims, cuts, low, high):
    factor_of = 1.0
    for axis_at, blocks in cuts:
        heights = jax.random.uniform(jax.random.fold_in(jax.random.fold_in(own_key, 6), axis_at), (blocks,), jnp.float32, low / len(cuts), high / len(cuts))
        factor_of = factor_of * jnp.repeat(jnp.exp(heights), dims[axis_at] // blocks).reshape((-1,) + (1,) * (len(dims) - 1 - axis_at))
    return factor_of


def centred(key, extent, spread, bound, cuts=(), kind=jnp.bfloat16):
    values = jax.random.normal(key, extent, jnp.float32) * spread
    if len(cuts) > 0:
        values = block_scale(key, extent, cuts, -0.22, 0.18) * values
    return jnp.clip(values, min=-bound, max=bound).astype(kind)


def setup_inputs(seed: int = 0) -> dict:
    key_of = jax.random.split(jax.random.key(seed), 11)
    block_input = centred(key_of[0], (SEQS, L, D), 1.0, 6.0, ((0, 4), (1, 8)), jnp.float32)
    segment_ids = draw_segment_ids(jax.random.fold_in(key_of[10], 71), 0)
    positions = draw_positions(jax.random.fold_in(key_of[10], 71), 0)
    attention_gain = jnp.clip(1.0 + 0.18 * jax.random.normal(key_of[3], (D,), jnp.float32), 0.099609375, 1.8984375).astype(jnp.bfloat16)
    feedforward_gain = jnp.clip(1.0 + 0.18 * jax.random.normal(key_of[4], (D,), jnp.float32), 0.099609375, 1.8984375).astype(jnp.bfloat16)
    qkv_weight = draw_qkv_weight(jax.random.fold_in(key_of[10], 71), 0)
    output_weight = centred(key_of[6], (D, D), (D // 16) ** -0.5, 0.75, ((0, 8), (1, 4)))
    expand_weight = centred(key_of[7], (D, 2, FF), D ** -0.5, 0.1875, ((0, 4), (2, 8)))
    contract_weight = centred(key_of[8], (FF, D), (FF // 4) ** -0.5, 0.25, ((0, 8), (1, 4)))
    cotangent = centred(key_of[9], (SEQS, L, D), 1.0, 6.0, ((0, 4), (1, 8)), jnp.float32)
    return {"block_input": block_input, "segment_ids": segment_ids, "positions": positions, "attention_gain": attention_gain, "feedforward_gain": feedforward_gain, "qkv_weight": qkv_weight, "output_weight": output_weight, "expand_weight": expand_weight, "contract_weight": contract_weight, "cotangent": cotangent}


EPSILON = 1e-05
MASKED = -1e+30
ROOT_HALF = 0.7071067811865476
DENSITY = 0.3989422804014327

def widen(tensor):
    return lax.optimization_barrier(tensor).astype(jnp.float32)

def layer_norm(values, gain_vector):
    centre = values - lax.optimization_barrier(jnp.mean(values, axis=-1, keepdims=True))
    variance = lax.optimization_barrier(jnp.mean(centre * centre, axis=-1, keepdims=True))
    inverse = lax.rsqrt(variance + EPSILON)
    normed = centre * inverse
    return (normed, inverse, (normed * gain_vector.astype(jnp.float32)).astype(jnp.bfloat16))

def norm_backward(upstream, normed, inverse, gain_vector):
    scaled = upstream * gain_vector.astype(jnp.float32)
    inner_term = scaled - lax.optimization_barrier(jnp.mean(scaled, axis=-1, keepdims=True)) - normed * lax.optimization_barrier(jnp.mean(scaled * normed, axis=-1, keepdims=True))
    return (inverse * inner_term, lax.optimization_barrier(jnp.sum(upstream * normed, axis=0)))

def gelu_pair(values):
    normal_cdf = 0.5 * (1.0 + lax.erf(values * ROOT_HALF))
    return (values * normal_cdf, normal_cdf + values * DENSITY * jnp.exp(-0.5 * values * values))

def rope_tables(places, head_size):
    half_size = head_size // 2
    frequency = jnp.exp(jnp.arange(half_size, dtype=jnp.float32) * (-2.0 * math.log(10000.0) / head_size))
    angles = places.astype(jnp.float32)[:, None] * frequency[None, :]
    cosine_table = jnp.concatenate([jnp.cos(angles), jnp.cos(angles)], axis=-1)[:, None, :]
    sine_table = jnp.concatenate([jnp.sin(angles), jnp.sin(angles)], axis=-1)[:, None, :]
    return (cosine_table, sine_table)

def rotate(tensor, cosine_table, sine_table):
    half_size = tensor.shape[-1] // 2
    turned = jnp.concatenate([-tensor[..., half_size:], tensor[..., :half_size]], axis=-1)
    return tensor * cosine_table + turned * sine_table

def unrotate(tensor, cosine_table, sine_table):
    half_size = tensor.shape[-1] // 2
    weighted = tensor * sine_table
    turned = jnp.concatenate([weighted[..., half_size:], -weighted[..., :half_size]], axis=-1)
    return tensor * cosine_table + turned

def block_scores(query_block, key_block, segment_query, segment_key, block_rows, scale):
    reach = WINDOW // 2
    scores = jnp.einsum('qhd,khd->hqk', widen(query_block), widen(key_block)) * scale
    offset = jnp.arange(block_rows)[:, None] + reach - jnp.arange(block_rows + 2 * reach)[None, :]
    valid = (jnp.abs(offset) <= reach) & (segment_query[:, None] == segment_key[None, :])
    return jnp.where(valid[None], scores, MASKED)

def band_pads(keys, values, segments):
    reach = WINDOW // 2
    pad_keys = jnp.pad(keys, ((reach, reach), (0, 0), (0, 0)))
    pad_values = jnp.pad(values, ((reach, reach), (0, 0), (0, 0)))
    pad_segments = jnp.pad(segments, (reach, reach), constant_values=-1)
    return (pad_keys, pad_values, pad_segments)

def band_forward(queries, keys, values, segments):
    length, heads, head_size = queries.shape
    reach = WINDOW // 2
    block = min(length, 512)
    scale = head_size ** (-0.5)
    pad_keys, pad_values, pad_segments = band_pads(keys, values, segments)

    def one_block(index):
        start = (index * block).astype(jnp.int32)
        query_block = lax.dynamic_slice_in_dim(queries, start, block, 0)
        key_block = lax.dynamic_slice_in_dim(pad_keys, start, block + 2 * reach, 0)
        value_block = lax.dynamic_slice_in_dim(pad_values, start, block + 2 * reach, 0)
        segment_query = lax.dynamic_slice_in_dim(segments, start, block, 0)
        segment_key = lax.dynamic_slice_in_dim(pad_segments, start, block + 2 * reach, 0)
        scores = block_scores(query_block, key_block, segment_query, segment_key, block, scale)
        peak = lax.optimization_barrier(jnp.max(scores, axis=-1, keepdims=True))
        log_total = peak + jnp.log(lax.optimization_barrier(jnp.sum(jnp.exp(scores - peak), axis=-1, keepdims=True)))
        weights = jnp.exp(scores - log_total).astype(jnp.bfloat16)
        context = jnp.einsum('hqk,khd->qhd', widen(weights), widen(value_block)).astype(jnp.bfloat16)
        return (context, log_total[..., 0])
    contexts, totals = lax.map(one_block, jnp.arange(length // block, dtype=jnp.int32))
    return (contexts.reshape(length, heads, head_size), totals)

def band_backward(queries, keys, values, segments, grad_context, totals):
    length, heads, head_size = queries.shape
    reach = WINDOW // 2
    block = min(length, 512)
    span = block + 2 * reach
    scale = head_size ** (-0.5)
    pad_keys, pad_values, pad_segments = band_pads(keys, values, segments)

    def one_block(carry, index):
        grad_keys, grad_values = carry
        start = (index * block).astype(jnp.int32)
        query_block = lax.dynamic_slice_in_dim(queries, start, block, 0)
        key_block = lax.dynamic_slice_in_dim(pad_keys, start, span, 0)
        value_block = lax.dynamic_slice_in_dim(pad_values, start, span, 0)
        segment_query = lax.dynamic_slice_in_dim(segments, start, block, 0)
        segment_key = lax.dynamic_slice_in_dim(pad_segments, start, span, 0)
        grad_block = lax.dynamic_slice_in_dim(grad_context, start, block, 0)
        scores = block_scores(query_block, key_block, segment_query, segment_key, block, scale)
        probs = jnp.exp(scores - totals[index][..., None])
        grad_probs = jnp.einsum('qhd,khd->hqk', widen(grad_block), widen(value_block))
        delta = lax.optimization_barrier(jnp.sum(probs * grad_probs, axis=-1, keepdims=True))
        grad_scores = (probs * (grad_probs - delta) * scale).astype(jnp.bfloat16)
        grad_query = jnp.einsum('hqk,khd->qhd', widen(grad_scores), widen(key_block))
        key_part = jnp.einsum('hqk,qhd->khd', widen(grad_scores), widen(query_block))
        value_part = jnp.einsum('hqk,qhd->khd', widen(probs.astype(jnp.bfloat16)), widen(grad_block))
        grad_keys = lax.dynamic_update_slice_in_dim(grad_keys, lax.dynamic_slice_in_dim(grad_keys, start, span, 0) + key_part, start, 0)
        grad_values = lax.dynamic_update_slice_in_dim(grad_values, lax.dynamic_slice_in_dim(grad_values, start, span, 0) + value_part, start, 0)
        return ((grad_keys, grad_values), grad_query)
    zeros = jnp.zeros((length + 2 * reach, heads, head_size), jnp.float32)
    (grad_keys, grad_values), grad_queries = lax.scan(one_block, (zeros, zeros), jnp.arange(length // block, dtype=jnp.int32))
    return (grad_queries.reshape(length, heads, head_size), grad_keys[reach:reach + length], grad_values[reach:reach + length])

def reference(block_input, segment_ids, positions, attention_gain, feedforward_gain, qkv_weight, output_weight, expand_weight, contract_weight, cotangent):
    qkv_matrix = qkv_weight.reshape(D, 3 * D)
    expand_matrix = expand_weight.reshape(D, 2 * FF)

    def sequence_pass(carry, items):
        grad_qkv, grad_output, grad_expand, grad_contract, gain_first, gain_second = carry
        tokens, segments, places, upstream = items
        cosine_table, sine_table = rope_tables(places, HD)
        normed_one, inverse_one, rows_one = layer_norm(tokens, attention_gain)
        projected = jnp.dot(rows_one, qkv_matrix, preferred_element_type=jnp.float32).reshape(L, 3, H, HD)
        queries = rotate(projected[:, 0], cosine_table, sine_table).astype(jnp.bfloat16)
        keys = rotate(projected[:, 1], cosine_table, sine_table).astype(jnp.bfloat16)
        values_in = projected[:, 2].astype(jnp.bfloat16)
        context, totals = band_forward(queries, keys, values_in, segments)
        context_rows = context.reshape(L, D)
        residual = tokens + jnp.dot(context_rows, output_weight, preferred_element_type=jnp.float32)
        normed_two, inverse_two, rows_two = layer_norm(residual, feedforward_gain)
        expanded = jnp.dot(rows_two, expand_matrix, preferred_element_type=jnp.float32).reshape(L, 2, FF)
        activated, slope = gelu_pair(expanded[:, 0])
        hidden = (activated * expanded[:, 1]).astype(jnp.bfloat16)
        result = residual + jnp.dot(hidden, contract_weight, preferred_element_type=jnp.float32)
        rows_back = upstream.astype(jnp.bfloat16)
        grad_contract = grad_contract + jnp.dot(hidden.T, rows_back, preferred_element_type=jnp.float32)
        grad_hidden = jnp.dot(rows_back, contract_weight.T, preferred_element_type=jnp.float32)
        grad_units = jnp.stack([grad_hidden * expanded[:, 1] * slope, grad_hidden * activated], axis=1).astype(jnp.bfloat16).reshape(L, 2 * FF)
        grad_expand = grad_expand + jnp.dot(rows_two.T, grad_units, preferred_element_type=jnp.float32)
        grad_two = jnp.dot(grad_units, expand_matrix.T, preferred_element_type=jnp.float32)
        through_two, gain_part = norm_backward(grad_two, normed_two, inverse_two, feedforward_gain)
        gain_second = gain_second + gain_part
        grad_mid = upstream + through_two
        rows_mid = grad_mid.astype(jnp.bfloat16)
        grad_output = grad_output + jnp.dot(context_rows.T, rows_mid, preferred_element_type=jnp.float32)
        grad_context = jnp.dot(rows_mid, output_weight.T, preferred_element_type=jnp.float32).astype(jnp.bfloat16).reshape(L, H, HD)
        grad_queries, grad_keys, grad_values = band_backward(queries, keys, values_in, segments, grad_context, totals)
        grad_proj = jnp.stack([unrotate(grad_queries, cosine_table, sine_table), unrotate(grad_keys, cosine_table, sine_table), grad_values], axis=1).astype(jnp.bfloat16).reshape(L, 3 * D)
        grad_qkv = grad_qkv + jnp.dot(rows_one.T, grad_proj, preferred_element_type=jnp.float32)
        grad_one = jnp.dot(grad_proj, qkv_matrix.T, preferred_element_type=jnp.float32)
        through_one, gain_part = norm_backward(grad_one, normed_one, inverse_one, attention_gain)
        gain_first = gain_first + gain_part
        return ((grad_qkv, grad_output, grad_expand, grad_contract, gain_first, gain_second), (result, grad_mid + through_one))
    start_carry = (jnp.zeros((D, 3 * D), jnp.float32), jnp.zeros((D, D), jnp.float32), jnp.zeros((D, 2 * FF), jnp.float32), jnp.zeros((FF, D), jnp.float32), jnp.zeros((D,), jnp.float32), jnp.zeros((D,), jnp.float32))
    final, stacked = lax.scan(sequence_pass, start_carry, (block_input, segment_ids, positions, cotangent))
    grad_qkv, grad_output, grad_expand, grad_contract, gain_first, gain_second = final
    return (stacked[0], stacked[1], gain_first, gain_second, grad_qkv.reshape(D, 3, D), grad_output, grad_expand.reshape(D, 2, FF), grad_contract)
```

```python
import functools
import math

import jax
import jax.numpy as jnp
from jax import lax
from jax.experimental import pallas as pl
from jax.experimental.pallas import tpu as pltpu
from jax.sharding import PartitionSpec as P

HD = 64
WINDOW = 128
REACH = WINDOW // 2
EPSILON = 1e-05
MASKED = -1e30
ROOT_HALF = 0.7071067811865476
DENSITY = 0.3989422804014327
NN = (((1,), (0,)), ((), ()))
NT = (((1,), (1,)), ((), ()))
TN = (((0,), (0,)), ((), ()))
F32, BF16 = jnp.float32, jnp.bfloat16
EX_A1, EX_UP, EX_Y, EX_A2, EX_DA, EX_OUT, EX_DY, EX_DX, EX_EDGE, EX_DEDGE = range(10)


def mm(left, right, dims):
    return lax.dot_general(left, right, dims, preferred_element_type=F32)


def norm_rows(values):
    centre = values - jnp.mean(values, axis=-1, keepdims=True)
    variance = jnp.mean(centre * centre, axis=-1, keepdims=True)
    inverse = lax.rsqrt(variance + EPSILON)
    return centre * inverse, inverse


def norm_back(upstream, normed, inverse, gain):
    scaled = upstream * gain
    inner = (
        scaled
        - jnp.mean(scaled, axis=-1, keepdims=True)
        - normed * jnp.mean(scaled * normed, axis=-1, keepdims=True)
    )
    return inverse * inner


def xor(value, k):
    bit, out = 1, value
    while bit <= k:
        if k & bit:
            out = out + bit * (1 - 2 * ((value // bit) % 2))
        bit *= 2
    return out


def xor_dynamic(value, k, count):
    bit, out = 1, 0
    while bit < count:
        out = out + bit * (((value // bit) + (k // bit)) % 2)
        bit *= 2
    return out


def children(k, count):
    low = (k & -k) if k else count
    bit, found = 1, []
    while bit < low:
        found.append(k + bit)
        bit *= 2
    return found


def turn(tensor, first_sign):
    half = HD // 2
    pieces = []
    for head in range(tensor.shape[1] // HD):
        low = tensor[:, head * HD : head * HD + half]
        high = tensor[:, head * HD + half : (head + 1) * HD]
        pieces += [-high, low] if first_sign < 0 else [high, -low]
    return jnp.concatenate(pieces, axis=1)


def blocks_of(tokens):
    size = min(tokens, 128)
    return [(start, size, size + 2 * REACH) for start in range(0, tokens, size)]


def layer_kernel(
    dps, tensors, units,
    x_ref, cot_ref, gain_ref, first_ref, feed_ref, cos_ref, sin_ref, segq_ref, segk_ref,
    out_ref, dx_ref, gg_ref, dfirst_ref, dfeed_ref,
    wa_ref, wf_ref, hd_ref,
    lca_ref, lcf_ref, lya_ref, lyf_ref, lza_ref, lzf_ref,
    gall_ref, gsum_ref, gland_ref,
    a1_ref, a2_ref, up_ref, dy_ref, acc_ref, da_ref,
    qkv_ref, ctx_ref, p_ref, dk_ref, dv_ref, dqkv_ref,
    sa_ref, ra_ref, sb_ref, rb_ref, hs_ref, hr_ref, es_ref, er_ref,
    zs, zr, ys, yr, cs, cr,
    rcs, rcr, rys, ryr, rzs, rzr,
    xs, xr, hss, hrs, gys, gyr, gcs, gcr, gss, gsr, ls,
):
    NY, NZ = dps // 2, tensors // 2
    dp, tensor = lax.axis_index("dp"), lax.axis_index("tensor")
    y, c = dp // 2, dp % 2
    z, x = tensor // 2, tensor % 2
    T, D = x_ref.shape
    rows = D // dps
    fold = first_ref.shape[1] // rows
    hw = first_ref.shape[0] * fold // 4
    UP = feed_ref.shape[0] * fold // 3
    heads = hw // HD
    ext = 2 * T + 2 * REACH
    scale = HD ** (-0.5)
    blocks = blocks_of(2 * T)

    ins = (first_ref, feed_ref)
    ws = (wa_ref, wf_ref)
    lcs, lys, lzs = (lca_ref, lcf_ref), (lya_ref, lyf_ref), (lza_ref, lzf_ref)

    def to_x():
        return dp, z * 2 + 1 - x

    def to_z(peer):
        return dp, peer * 2 + x

    def to_y(j):
        return xor(y, j) * 2 + c, tensor

    def to_c():
        return y * 2 + 1 - c, tensor

    def remote(src, dst, send, recv, device):
        return pltpu.make_async_remote_copy(
            src_ref=src, dst_ref=dst, send_sem=send, recv_sem=recv,
            device_id=device, device_id_type=pl.DeviceIdType.MESH,
        )

    def zcopy(lane, k):
        low = k & -k
        rest = k ^ low
        there = ws[lane].at[xor(z, rest), c, y]
        return remote(
            ins[lane] if rest == 0 else there, there, zs.at[lane, k], zr.at[lane, k], to_z(xor(z, low))
        )

    def ycopy(lane, k, j):
        there = ws[lane].at[xor(z, k), c, y]
        return remote(ins[lane] if k == 0 else there, there, ys.at[lane, k, j], yr.at[lane, k, j], to_y(j))

    def ccopy(lane, k, j):
        there = ws[lane].at[xor(z, k), c, xor(y, j)]
        own = k == 0 and j == 0
        return remote(ins[lane] if own else there, there, cs.at[lane, k, j], cr.at[lane, k, j], to_c())

    def zstart(lane):
        for k in range(1, NZ):
            if k & (k - 1) == 0:
                zcopy(lane, k).start()

    def zpass(lane, k):
        if k:
            zcopy(lane, k).wait_recv()
            for child in children(k, NZ):
                zcopy(lane, child).start()
        for j in range(1, NY):
            ycopy(lane, k, j).start()
        ccopy(lane, k, 0).start()

    def ypass(lane, k):
        for j in range(1, NY):
            ycopy(lane, k, j).wait_recv()
            ccopy(lane, k, j).start()

    def cpass(lane, k):
        for j in range(NY):
            ccopy(lane, k, j).wait_recv()

    def sent(lane, k):
        for child in children(k, NZ):
            zcopy(lane, child).wait_send()
        for j in range(NY):
            if j:
                ycopy(lane, k, j).wait_send()
            ccopy(lane, k, j).wait_send()

    def rccopy(lane, k):
        t = xor(z, k)
        return remote(ws[lane].at[t, 1 - c], lcs[lane].at[t], rcs.at[lane, k], rcr.at[lane, k], to_c())

    def rycopy(lane, k, j):
        t = xor(z, k)
        return remote(
            ws[lane].at[t, c, xor(y, j)], lys[lane].at[k, j - 1], rys.at[lane, k, j], ryr.at[lane, k, j], to_y(j)
        )

    def rzcopy(lane, k):
        low = k & -k
        return remote(
            ws[lane].at[xor(z, k), c, y], lzs[lane].at[k - 1], rzs.at[lane, k], rzr.at[lane, k], to_z(xor(z, low))
        )

    def r0(lane, k):
        rccopy(lane, k).start()

    def r1(lane, k):
        t = xor(z, k)
        rccopy(lane, k).wait_recv()
        dw, land = ws[lane], lcs[lane]

        def one(j, carry):
            dw[t, c, j] = (dw[t, c, j].astype(F32) + land[t, j].astype(F32)).astype(BF16)
            return carry

        lax.fori_loop(0, NY, one, 0)
        for j in range(1, NY):
            rycopy(lane, k, j).start()

    def r2(lane, k):
        t = xor(z, k)
        total = ws[lane][t, c, y].astype(F32)
        for j in range(1, NY):
            rycopy(lane, k, j).wait_recv()
            total = total + lys[lane][k, j - 1].astype(F32)
        for child in children(k, NZ):
            rzcopy(lane, child).wait_recv()
            total = total + lzs[lane][child - 1].astype(F32)
        if k == 0:
            (dfirst_ref, dfeed_ref)[lane][...] = total
        else:
            ws[lane][t, c, y] = total.astype(BF16)
            rzcopy(lane, k).start()

    own_rows = pl.ds(pl.multiple_of(x * T, T), T)
    other_rows = pl.ds(pl.multiple_of((1 - x) * T, T), T)
    own_ext = pl.ds(pl.multiple_of(REACH + x * T, REACH), T)

    edge_ext = pl.ds(pl.multiple_of(REACH + x * (2 * T - REACH), REACH), REACH)
    rest_ext = pl.ds(pl.multiple_of(REACH + REACH * (1 - x) + x * T, REACH), T - REACH)

    def share(ref, which, place):
        return remote(ref.at[place], ref.at[place], xs.at[which], xr.at[which], to_x())

    def swap(send, recv, which):
        return remote(send, recv, xs.at[which], xr.at[which], to_x())

    def piece(lane, t, d, lo, hi):
        if fold == 1:
            return ws[lane][t, d % 2, d // 2, lo:hi, :]
        slab = ws[lane][t, d % 2, d // 2]
        return jnp.concatenate([slab[:, f * rows : (f + 1) * rows] for f in range(fold)], axis=0)[lo:hi]

    def wide(lane, t, lo, hi):
        return jnp.concatenate([piece(lane, t, d, lo, hi) for d in range(dps)], axis=1)

    def put(lane, t, d, upper, lower):
        cut = upper.shape[0]
        if fold == 1:
            ws[lane][t, d % 2, d // 2, :cut, :] = upper.astype(BF16)
            ws[lane][t, d % 2, d // 2, cut:, :] = lower.astype(BF16)
            return
        slab = jnp.concatenate([upper, lower], axis=0)
        high = slab.shape[0] // fold
        slab = jnp.concatenate([slab[f * high : (f + 1) * high] for f in range(fold)], axis=1)
        ws[lane][t, d % 2, d // 2] = slab.astype(BF16)

    loads = [
        pltpu.make_async_copy(x_ref, out_ref, ls.at[0]),
        pltpu.make_async_copy(cot_ref, dx_ref, ls.at[1]),
        pltpu.make_async_copy(first_ref, wa_ref.at[z, c, y], ls.at[2]),
        pltpu.make_async_copy(feed_ref, wf_ref.at[z, c, y], ls.at[3]),
    ]
    x_again = pltpu.make_async_copy(x_ref, da_ref.at[pl.ds(0, T)], ls.at[4])
    for load in loads:
        load.start()
    barrier = pltpu.get_barrier_semaphore()
    peers = [to_x(), to_c()] + [to_y(j) for j in range(1, NY)] + [to_z(xor(z, k)) for k in range(1, NZ)]
    for peer in peers:
        pl.semaphore_signal(barrier, inc=1, device_id=peer, device_id_type=pl.DeviceIdType.MESH)
    pl.semaphore_wait(barrier, len(peers))

    def gycopy(j):
        return remote(gain_ref, gall_ref.at[dp], gys.at[j], gyr.at[j], to_y(j))

    def gccopy(j):
        own = gall_ref.at[xor(y, j) * 2 + c]
        return remote(gain_ref if j == 0 else own, own, gcs.at[j], gcr.at[j], to_c())

    for j in range(1, NY):
        gycopy(j).start()
    gccopy(0).start()
    zstart(0)
    zpass(0, 0)
    gall_ref[dp] = gain_ref[...]
    loads[0].wait()
    normed, _ = norm_rows(out_ref[...])
    for j in range(1, NY):
        gycopy(j).wait_recv()
        gccopy(j).start()
    for j in range(NY):
        gccopy(j).wait_recv()

    def gain_row(which):
        return jnp.concatenate([gall_ref[d, which : which + 1, :] for d in range(dps)], axis=1)

    a1_ref[own_ext, :] = (normed * gain_row(0)).astype(BF16)
    share(a1_ref, EX_EDGE, edge_ext).start()
    share(a1_ref, EX_A1, rest_ext).start()
    loads[1].wait()
    up_ref[own_rows, :] = dx_ref[...].astype(BF16)
    loads[2].wait()
    loads[3].wait()
    dqkv_ref[...] = jnp.zeros_like(dqkv_ref)
    edge = jnp.zeros((REACH, D), BF16)

    @pl.when(z == 0)
    def _():
        a1_ref[:REACH, :] = edge

    @pl.when(z == NZ - 1)
    def _():
        a1_ref[ext - REACH :, :] = edge

    def halo(which, send, recv):
        peer = z - 1 if which == 0 else z + 1
        return remote(send, recv, hss.at[which], hrs.at[which], to_z(peer))

    def halo_a(which):
        if which == 0:
            return halo(0, a1_ref.at[pl.ds(REACH, REACH)], a1_ref.at[pl.ds(ext - REACH, REACH)])
        return halo(1, a1_ref.at[pl.ds(2 * T, REACH)], a1_ref.at[pl.ds(0, REACH)])

    def halo_d(which):
        peer = z - 1 if which == 0 else z + 1
        return remote(hs_ref.at[which], hr_ref.at[1 - which], hss.at[2 + which], hrs.at[2 + which], to_z(peer))

    def halo_start(maker):
        @pl.when(z > 0)
        def _():
            maker(0).start()

        @pl.when(z < NZ - 1)
        def _():
            maker(1).start()

    def halo_wait(maker):
        @pl.when(z > 0)
        def _():
            maker(1).wait_recv()

        @pl.when(z < NZ - 1)
        def _():
            maker(0).wait_recv()

    def halo_sent(maker):
        @pl.when(z > 0)
        def _():
            maker(0).wait_send()

        @pl.when(z < NZ - 1)
        def _():
            maker(1).wait_send()

    share(a1_ref, EX_EDGE, edge_ext).wait_recv()
    halo_start(halo_a)
    zpass(0, 1)
    zstart(1)
    ypass(0, 0)
    zpass(0, 2)
    ypass(0, 1)
    share(a1_ref, EX_A1, rest_ext).wait_recv()
    share(up_ref, EX_UP, own_rows).start()
    halo_wait(halo_a)

    def band(start, size, span):
        row = lax.broadcasted_iota(jnp.int32, (size, span), 0)
        col = lax.broadcasted_iota(jnp.int32, (size, span), 1)
        near = jnp.abs(row + REACH - col) <= REACH
        return near & (segq_ref[start : start + size, :] == segk_ref[:, start : start + span])

    def at_tick(i, count, act):
        for tick in range(count):
            @pl.when(i == tick)
            def _(tick=tick):
                act(tick)

    def attend(i, carry):
        def control(tick):
            if tick and tick + 2 < NZ:
                zpass(0, tick + 2)
            if tick >= NZ - 2:
                zpass(1, tick + 2 - NZ)
            if tick >= 2:
                ypass(0, tick)
            cpass(0, tick)

        at_tick(i, NZ, control)
        t = xor_dynamic(z, i, NZ)
        qkv = mm(a1_ref[...], wide(0, t, 0, 3 * hw), NT)
        cos, sin = cos_ref[...], sin_ref[...]
        q, k, v = qkv[:, :hw], qkv[:, hw : 2 * hw], qkv[:, 2 * hw :].astype(BF16)
        q = (q * cos + turn(q, -1) * sin).astype(BF16)
        k = (k * cos + turn(k, -1) * sin).astype(BF16)
        qkv_ref[i, 0], qkv_ref[i, 1], qkv_ref[i, 2] = q, k, v
        for b, (start, size, span) in enumerate(blocks):
            valid = band(start, size, span)
            contexts = []
            for head in range(heads):
                lanes = slice(head * HD, (head + 1) * HD)
                qb = q[REACH + start : REACH + start + size, lanes]
                kb = k[start : start + span, lanes]
                vb = v[start : start + span, lanes]
                s = jnp.where(valid, mm(qb, kb, NT) * scale, MASKED)
                e = jnp.exp(s - jnp.max(s, axis=-1, keepdims=True))
                weights = (e * (1.0 / jnp.sum(e, axis=-1, keepdims=True))).astype(BF16)
                p_ref[i, b, head] = weights
                contexts.append(mm(weights, vb, NN))
            ctx_ref[i, start : start + size, :] = jnp.concatenate(contexts, axis=1).astype(BF16)
        return carry

    lax.fori_loop(0, NZ, attend, 0)

    def project(place):
        total = 0.0
        for i in range(NZ):
            total = total + mm(ctx_ref[i, place, :], wide(0, xor(z, i), 3 * hw, 4 * hw), NN)
        return total

    sa_ref[...] = project(other_rows).astype(BF16)
    swap(sa_ref, ra_ref, EX_Y).start()
    out_ref[...] += project(own_rows)
    ypass(1, 0)
    zpass(1, 2)
    swap(sa_ref, ra_ref, EX_Y).wait()
    out_ref[...] += ra_ref[...].astype(F32)
    normed, _ = norm_rows(out_ref[...])
    a2_ref[own_rows, :] = (normed * gain_row(1)).astype(BF16)
    share(a2_ref, EX_A2, own_rows).start()
    share(up_ref, EX_UP, own_rows).wait_recv()
    acc = acc_ref.at[pl.ds(0, 2 * T)]
    acc[...] = jnp.zeros((2 * T, D), F32)
    da_ref[...] = jnp.zeros_like(da_ref)

    HALF, GRAD = 0, 1
    OWN, OTHER = 0, 1
    steps = [(HALF, 0, OWN), (HALF, 1, OWN), (HALF, 0, OTHER), (GRAD, 0, 0), (HALF, 1, OTHER)]
    for k in range(2, NZ):
        steps += [(HALF, k, OTHER), (HALF, k, OWN)]
    steps += [(GRAD, k, 0) for k in range(NZ - 1, 0, -1)]

    def table(step, column):
        out = 0
        for at, row in enumerate(steps):
            if row[column]:
                out = out + row[column] * (step == at).astype(jnp.int32)
        return out

    def before(at):
        kind, k, side = steps[at]
        if kind == GRAD:
            sent(1, k)
            return
        if (k, side) == (1, OWN):
            ypass(1, 1)
            zpass(1, 3)
        if (k, side) == (0, OTHER):
            share(a2_ref, EX_A2, own_rows).wait_recv()
        if (k, side) == (1, OTHER):
            ypass(1, 2)
        if k >= 2 and side == OTHER:
            if k + 2 < NZ:
                zpass(1, k + 2)
            if k > 2:
                ypass(1, k)
            cpass(1, k)
        if k < 2 and side == OWN:
            cpass(1, k)

    def after(at):
        kind, k, side = steps[at]
        if kind == GRAD:
            r0(1, k)
            if 0 < k < NZ - 1:
                r1(1, k + 1)
        elif (k, side) == (2, OTHER):
            r1(1, 0)
        elif (k, side) == (NZ - 1, OTHER):
            sa_ref[...] = da_ref[other_rows, :].astype(BF16)
            swap(sa_ref, ra_ref, EX_DA).start()

    def feed(step, carry):
        at_tick(step, len(steps), before)
        k = table(step, 1)
        t = xor_dynamic(z, k, NZ)
        kind = table(step, 0)

        @pl.when(kind == HALF)
        def _():
            side = table(step, 2)
            place = pl.ds(pl.multiple_of((x + side - 2 * x * side) * T, T), T)
            a, up = a2_ref[place, :], up_ref[place, :]
            u01 = mm(wide(1, t, 0, 2 * UP), a, NT)
            dg = mm(wide(1, t, 2 * UP, 3 * UP), up, NT)
            u0, u1 = u01[:UP], u01[UP:]
            cdf = 0.5 * (1.0 + lax.erf(u0 * ROOT_HALF))
            activated = u0 * cdf
            slope = cdf + u0 * DENSITY * jnp.exp(-0.5 * u0 * u0)
            hidden = (activated * u1).astype(BF16)
            du = jnp.concatenate([dg * u1 * slope, dg * activated], axis=0).astype(BF16)
            hd_ref[k, side, : 2 * UP, :] = du
            hd_ref[k, side, 2 * UP :, :] = hidden
            hidden_t, du_t = hidden.T, du.T
            for d in range(dps):
                cols = slice(d * rows, (d + 1) * rows)
                da_ref[place, cols] += mm(du_t, piece(1, t, d, 0, 2 * UP), NN)
                acc[place, cols] += mm(hidden_t, piece(1, t, d, 2 * UP, 3 * UP), NN)

        @pl.when(kind == GRAD)
        def _():
            mine, theirs = hd_ref[k, 0], hd_ref[k, 1]
            for d in range(dps):
                cols = slice(d * rows, (d + 1) * rows)
                upper = mm(mine[: 2 * UP], a2_ref[own_rows, cols], NN)
                upper = upper + mm(theirs[: 2 * UP], a2_ref[other_rows, cols], NN)
                lower = mm(mine[2 * UP :], up_ref[own_rows, cols], NN)
                lower = lower + mm(theirs[2 * UP :], up_ref[other_rows, cols], NN)
                put(1, t, d, upper, lower)

        at_tick(step, len(steps), after)
        return carry

    lax.fori_loop(0, len(steps), feed, 0)

    sb_ref[...] = acc[other_rows, :].astype(BF16)
    swap(sa_ref, ra_ref, EX_DA).wait()
    da_own = da_ref[own_rows, :] + ra_ref[...].astype(F32)
    normed, inverse = norm_rows(out_ref[...])
    dx_ref[...] += norm_back(da_own, normed, inverse, gain_row(1))
    dy_ref[own_rows, :] = dx_ref[...].astype(BF16)
    share(dy_ref, EX_DY, own_rows).start()
    r1(1, 1)
    gain_two = jnp.sum(da_own * normed, axis=0, keepdims=True)
    x_again.start()
    out_ref[...] += acc[own_rows, :]
    acc_ref[...] = jnp.zeros_like(acc_ref)
    r2(1, NZ - 1)
    share(dy_ref, EX_DY, own_rows).wait_recv()
    swap(sb_ref, rb_ref, EX_OUT).start()

    inner = slice(REACH, REACH + 2 * T)

    def attend_back(step, carry):
        i = NZ - 1 - step
        t = xor_dynamic(z, i, NZ)
        dyb = dy_ref[...]
        dc = mm(dyb, wide(0, t, 3 * hw, 4 * hw), NT).astype(BF16)
        dk_ref[...] = jnp.zeros_like(dk_ref)
        dv_ref[...] = jnp.zeros_like(dv_ref)
        dq_rows = []
        for b, (start, size, span) in enumerate(blocks):
            dq_parts, dk_parts, dv_parts = [], [], []
            for head in range(heads):
                lanes = slice(head * HD, (head + 1) * HD)
                qb = qkv_ref[i, 0, REACH + start : REACH + start + size, lanes]
                kb = qkv_ref[i, 1, start : start + span, lanes]
                vb = qkv_ref[i, 2, start : start + span, lanes]
                db = dc[start : start + size, lanes]
                weights = p_ref[i, b, head]
                probs = weights.astype(F32)
                dpr = mm(db, vb, NT)
                delta = jnp.sum(probs * dpr, axis=-1, keepdims=True)
                ds = (probs * (dpr - delta) * scale).astype(BF16)
                dq_parts.append(mm(ds, kb, NN))
                dk_parts.append(mm(ds, qb, TN))
                dv_parts.append(mm(weights, db, TN))
            dq_rows.append(jnp.concatenate(dq_parts, axis=1))
            dk_ref[start : start + span, :] += jnp.concatenate(dk_parts, axis=1)
            dv_ref[start : start + span, :] += jnp.concatenate(dv_parts, axis=1)
        cos, sin = cos_ref[...], sin_ref[...]
        dq = jnp.concatenate(dq_rows, axis=0)
        dk = dk_ref[...]
        dqkv_ref[inner, :hw] = (dq * cos[inner] + turn(dq * sin[inner], 1)).astype(BF16)
        dqkv_ref[:, hw : 2 * hw] = (dk * cos + turn(dk * sin, 1)).astype(BF16)
        dqkv_ref[:, 2 * hw :] = dv_ref[...].astype(BF16)
        acc_ref[...] += mm(dqkv_ref[...], wide(0, t, 0, 3 * hw), NN)
        dqkv_t, ctx_t = dqkv_ref[...].T, ctx_ref[i].T
        for d in range(dps):
            cols = slice(d * rows, (d + 1) * rows)
            put(0, t, d, mm(dqkv_t, a1_ref[:, cols], NN), mm(ctx_t, dy_ref[:, cols], NN))

        def control(tick):
            k = NZ - 1 - tick
            r0(0, k)
            if k + 1 < NZ:
                r1(0, k + 1)
            if tick == 1:
                r2(1, NZ - 2)
            if tick == 3:
                r2(1, NZ - 3)

        at_tick(step, NZ, control)
        return carry

    for k in range(NZ):
        sent(0, k)
    lax.fori_loop(0, NZ, attend_back, 0)

    hs_ref[0] = acc_ref[:REACH, :].astype(BF16)
    hs_ref[1] = acc_ref[ext - REACH :, :].astype(BF16)
    halo_start(halo_d)
    swap(sb_ref, rb_ref, EX_OUT).wait()
    out_ref[...] += rb_ref[...].astype(F32)
    bulk = pl.ds(pl.multiple_of(REACH + REACH * x + (1 - x) * T, REACH), T - REACH)
    sa_ref[: T - REACH, :] = acc_ref[bulk, :].astype(BF16)
    bulk_out = swap(sa_ref.at[pl.ds(0, T - REACH)], ra_ref.at[pl.ds(0, T - REACH)], EX_DX)
    bulk_out.start()
    r1(0, 0)
    gain_one = jnp.sum(acc_ref[...] * a1_ref[...].astype(F32), axis=0, keepdims=True) / gain_row(0)
    for d in range(dps):
        cols = slice(d * rows, (d + 1) * rows)
        gsum_ref[d] = jnp.concatenate(
            [gain_one[:, cols], gain_two[:, cols], jnp.zeros((6, rows), F32)], axis=0
        )
    stages = [to_x(), to_c()]
    stages += [to_y(2**b) for b in range(NY.bit_length() - 1)]
    stages += [to_z(xor(z, 2**b)) for b in range(NZ.bit_length() - 1)]

    def gcopy(s):
        return remote(gsum_ref, gland_ref.at[s], gss.at[s], gsr.at[s], stages[s])

    def gain_stage(s):
        gcopy(s).wait()
        gsum_ref[...] += gland_ref[s]
        if s + 1 < len(stages):
            gcopy(s + 1).start()

    gcopy(0).start()
    halo_wait(halo_d)

    @pl.when(z > 0)
    def _():
        acc_ref[REACH : 2 * REACH, :] += hr_ref[0].astype(F32)

    @pl.when(z < NZ - 1)
    def _():
        acc_ref[ext - 2 * REACH : ext - REACH, :] += hr_ref[1].astype(F32)

    far_edge = pl.ds(pl.multiple_of(REACH + (1 - x) * (2 * T - REACH), REACH), REACH)
    es_ref[...] = acc_ref[far_edge, :].astype(BF16)
    swap(es_ref, er_ref, EX_DEDGE).start()
    gain_stage(0)
    r2(0, NZ - 1)
    gain_stage(1)
    gain_stage(2)
    for k in range(NZ - 2, 1, -1):
        r2(0, k)
    gain_stage(3)
    x_again.wait()
    normed, inverse = norm_rows(da_ref[:T, :])
    bulk_out.wait()
    swap(es_ref, er_ref, EX_DEDGE).wait()
    acc_ref[rest_ext, :] += ra_ref[: T - REACH, :].astype(F32)
    acc_ref[edge_ext, :] += er_ref[...].astype(F32)
    dx_ref[...] += norm_back(acc_ref[own_ext, :], normed, inverse, gain_row(0))
    r2(0, 1)
    for s in range(4, len(stages)):
        gain_stage(s)
    gg_ref[...] = gsum_ref[dp]
    for k in range(NZ - 4, 0, -1):
        r2(1, k)
    r2(1, 0)
    r2(0, 0)

    for j in range(1, NY):
        gycopy(j).wait_send()
    for j in range(NY):
        gccopy(j).wait_send()
    for lane in range(2):
        for k in range(NZ):
            if k:
                rzcopy(lane, k).wait_send()
            for j in range(1, NY):
                rycopy(lane, k, j).wait_send()
            rccopy(lane, k).wait_send()
    share(a1_ref, EX_EDGE, edge_ext).wait_send()
    share(a1_ref, EX_A1, rest_ext).wait_send()
    share(up_ref, EX_UP, own_rows).wait_send()
    share(a2_ref, EX_A2, own_rows).wait_send()
    share(dy_ref, EX_DY, own_rows).wait_send()
    halo_sent(halo_a)
    halo_sent(halo_d)


def body(
    dps,
    tensors,
    block_input,
    segment_ids,
    positions,
    attention_gain,
    feedforward_gain,
    qkv_weight,
    output_weight,
    expand_weight,
    contract_weight,
    cotangent,
):
    T, D = block_input.shape[1:]
    rows = qkv_weight.shape[0]
    hw = qkv_weight.shape[2]
    units = contract_weight.shape[0]
    fold = max(1, 128 // rows)
    UP = -(-units // (8 * fold)) * 8 * fold
    heads = hw // HD
    ext = 2 * T + 2 * REACH
    NY, NZ = dps // 2, tensors // 2

    pair = lax.axis_index("tensor") // 2
    seg_all = jnp.pad(segment_ids[0], (REACH, REACH), constant_values=-1)
    pos_all = jnp.pad(positions[0], (REACH, REACH))
    seg_k = lax.dynamic_slice_in_dim(seg_all, pair * 2 * T, ext, 0)
    pos = lax.dynamic_slice_in_dim(pos_all, pair * 2 * T, ext, 0)
    seg_q = seg_k[REACH : REACH + 2 * T]
    half = HD // 2
    frequency = jnp.exp(jnp.arange(half, dtype=F32) * (-2.0 * math.log(10000.0) / HD))
    angles = pos.astype(F32)[:, None] * frequency[None, :]
    cos = jnp.tile(jnp.cos(angles), (1, 2 * heads))
    sin = jnp.tile(jnp.sin(angles), (1, 2 * heads))

    gains = jnp.pad(jnp.stack([attention_gain, feedforward_gain]).astype(F32), ((0, 6), (0, 0)))
    first = jnp.concatenate(
        [jnp.transpose(qkv_weight, (1, 2, 0)).reshape(3 * hw, rows), output_weight], axis=0
    )
    stacked = jnp.concatenate([jnp.transpose(expand_weight, (1, 2, 0)), contract_weight[None]], axis=0)
    stacked = jnp.pad(stacked, ((0, 0), (0, UP - units), (0, 0))).reshape(3 * UP, rows)

    def folded(slab):
        high = slab.shape[0] // fold
        return jnp.concatenate([slab[f * high : (f + 1) * high] for f in range(fold)], axis=1)

    def unfolded(slab):
        return jnp.concatenate([slab[:, f * rows : (f + 1) * rows] for f in range(fold)], axis=0)

    if fold > 1:
        first, stacked = folded(first), folded(stacked)
    blocks = blocks_of(2 * T)
    size, span = blocks[0][1:]
    n_stage = 2 + (NY.bit_length() - 1) + (NZ.bit_length() - 1)
    vm, dma = pltpu.VMEM, pltpu.SemaphoreType.DMA
    fa, ff = first.shape, stacked.shape
    ny1, nz1 = max(NY - 1, 1), max(NZ - 1, 1)
    scratch = [
        vm((NZ, 2, NY) + fa, BF16), vm((NZ, 2, NY) + ff, BF16), vm((NZ, 2, 3 * UP, T), BF16),
        vm((NZ, NY) + fa, BF16), vm((NZ, NY) + ff, BF16),
        vm((NZ, ny1) + fa, BF16), vm((NZ, ny1) + ff, BF16),
        vm((nz1,) + fa, BF16), vm((nz1,) + ff, BF16),
        vm((dps, 8, rows), F32), vm((dps, 8, rows), F32), vm((n_stage, dps, 8, rows), F32),
        vm((ext, D), BF16), vm((2 * T, D), BF16), vm((2 * T, D), BF16), vm((2 * T, D), BF16),
        vm((ext, D), F32), vm((2 * T, D), F32),
        vm((NZ, 3, ext, hw), BF16), vm((NZ, 2 * T, hw), BF16),
        vm((NZ, len(blocks), heads, size, span), BF16),
        vm((ext, hw), F32), vm((ext, hw), F32), vm((ext, 3 * hw), BF16),
        vm((T, D), BF16), vm((T, D), BF16), vm((T, D), BF16), vm((T, D), BF16),
        vm((2, REACH, D), BF16), vm((2, REACH, D), BF16), vm((REACH, D), BF16), vm((REACH, D), BF16),
        dma((2, NZ)), dma((2, NZ)), dma((2, NZ, NY)), dma((2, NZ, NY)), dma((2, NZ, NY)), dma((2, NZ, NY)),
        dma((2, NZ)), dma((2, NZ)), dma((2, NZ, NY)), dma((2, NZ, NY)), dma((2, NZ)), dma((2, NZ)),
        dma((10,)), dma((10,)), dma((4,)), dma((4,)),
        dma((NY,)), dma((NY,)), dma((NY,)), dma((NY,)), dma((n_stage,)), dma((n_stage,)), dma((5,)),
    ]
    out, dx, gg, dfirst, dfeed = pl.pallas_call(
        functools.partial(layer_kernel, dps, tensors, units),
        in_specs=[
            pl.BlockSpec(memory_space=pl.ANY if i in (0, 1, 3, 4) else pltpu.VMEM) for i in range(9)
        ],
        out_specs=[pl.BlockSpec(memory_space=pltpu.VMEM)] * 5,
        out_shape=[
            jax.ShapeDtypeStruct((T, D), F32),
            jax.ShapeDtypeStruct((T, D), F32),
            jax.ShapeDtypeStruct((8, rows), F32),
            jax.ShapeDtypeStruct(fa, F32),
            jax.ShapeDtypeStruct(ff, F32),
        ],
        scratch_shapes=scratch,
        compiler_params=pltpu.CompilerParams(
            collective_id=0, has_side_effects=True, vmem_limit_bytes=63 * 1024 * 1024
        ),
        name="layer",
    )(block_input[0], cotangent[0], gains, first, stacked, cos, sin, seg_q[:, None], seg_k[None, :])

    if fold > 1:
        dfirst, dfeed = unfolded(dfirst), unfolded(dfeed)
    dqkv = dfirst[: 3 * hw].reshape(3, hw, rows)
    dfeed = dfeed.reshape(3, UP, rows)[:, :units]
    return (
        out[None],
        dx[None],
        gg[0],
        gg[1],
        jnp.transpose(dqkv, (2, 0, 1)),
        dfirst[3 * hw :],
        jnp.transpose(dfeed[:2], (2, 0, 1)),
        dfeed[2],
    )


def solution(mesh):
    return jax.shard_map(
        functools.partial(body, mesh.shape["dp"], mesh.shape["tensor"]),
        mesh=mesh,
        in_specs=(
            P("dp", "tensor", None),
            P("dp", None),
            P("dp", None),
            P("dp"),
            P("dp"),
            P("dp", None, "tensor"),
            P("tensor", "dp"),
            P("dp", None, "tensor"),
            P("tensor", "dp"),
            P("dp", "tensor", None),
        ),
        out_specs=(
            P("dp", "tensor", None),
            P("dp", "tensor", None),
            P("dp"),
            P("dp"),
            P("dp", None, "tensor"),
            P("tensor", "dp"),
            P("dp", None, "tensor"),
            P("tensor", "dp"),
        ),
        check_vma=False,
    )
```

```python
import functools
import math

import jax
import jax.numpy as jnp
from jax import lax
from jax.experimental import pallas as pl
from jax.experimental.pallas import tpu as pltpu
from jax.sharding import PartitionSpec as P

HD = 64
WINDOW = 128
REACH = WINDOW // 2
EPSILON = 1e-05
MASKED = -1e30
ROOT_HALF = 0.7071067811865476
DENSITY = 0.3989422804014327
NN = (((1,), (0,)), ((), ()))
NT = (((1,), (1,)), ((), ()))
TN = (((0,), (0,)), ((), ()))
F32, BF16 = jnp.float32, jnp.bfloat16
EX_A1, EX_UP, EX_OUT, EX_DX, EX_EDGE, EX_DEDGE = range(6)
EX_Y, EX_A2, EX_DA, EX_DY = 6, 8, 10, 12


def mm(left, right, dims):
    return lax.dot_general(left, right, dims, preferred_element_type=F32)


def norm_rows(values):
    centre = values - jnp.mean(values, axis=-1, keepdims=True)
    variance = jnp.mean(centre * centre, axis=-1, keepdims=True)
    inverse = lax.rsqrt(variance + EPSILON)
    return centre * inverse, inverse


def norm_back(upstream, normed, inverse, gain):
    scaled = upstream * gain
    inner = (
        scaled
        - jnp.mean(scaled, axis=-1, keepdims=True)
        - normed * jnp.mean(scaled * normed, axis=-1, keepdims=True)
    )
    return inverse * inner


def xor(value, k):
    bit, out = 1, value
    while bit <= k:
        if k & bit:
            out = out + bit * (1 - 2 * ((value // bit) % 2))
        bit *= 2
    return out


def xor_dynamic(value, k, count):
    bit, out = 1, 0
    while bit < count:
        out = out + bit * (((value // bit) + (k // bit)) % 2)
        bit *= 2
    return out


def children(k, count):
    low = (k & -k) if k else count
    bit, found = 1, []
    while bit < low:
        found.append(k + bit)
        bit *= 2
    return found


def turn(tensor, first_sign):
    half = HD // 2
    pieces = []
    for head in range(tensor.shape[1] // HD):
        low = tensor[:, head * HD : head * HD + half]
        high = tensor[:, head * HD + half : (head + 1) * HD]
        pieces += [-high, low] if first_sign < 0 else [high, -low]
    return jnp.concatenate(pieces, axis=1)


def blocks_of(tokens):
    size = min(tokens, 128)
    return [(start, size, size + 2 * REACH) for start in range(0, tokens, size)]


def layer_kernel(
    dps, tensors, units,
    x_ref, cot_ref, gain_ref, first_ref, feed_ref, cos_in, sin_in, segq_in, segk_ref,
    out_ref, dx_ref, gg_ref, dfirst_ref, dfeed_ref,
    cos_ref, sin_ref, segq_ref, wa_ref, wf_ref, hd_ref,
    lca_ref, lcf_ref, lya_ref, lyf_ref, lza_ref, lzf_ref,
    gall_ref, gsum_ref, gland_ref,
    a1_ref, a2_ref, up_ref, dy_ref, acc_ref, da_ref,
    qkv_ref, ctx_ref, p_ref, dk_ref, dv_ref, dqkv_ref,
    sa_ref, ra_ref, sb_ref, rb_ref, hs_ref, hr_ref, es_ref, er_ref,
    zs, zr, ys, yr, cs, cr,
    rcs, rcr, rys, ryr, rzs, rzr,
    xs, xr, hss, hrs, gys, gyr, gcs, gcr, gss, gsr, ls,
):
    NY, NZ = dps // 2, tensors // 2
    dp, tensor = lax.axis_index("dp"), lax.axis_index("tensor")
    y, c = dp // 2, dp % 2
    z, x = tensor // 2, tensor % 2
    T, D = x_ref.shape
    rows = D // dps
    fold = first_ref.shape[1] // rows
    hw = first_ref.shape[0] * fold // 4
    UP = feed_ref.shape[0] * fold // 3
    heads = hw // HD
    ext = 2 * T + 2 * REACH
    scale = HD ** (-0.5)
    blocks = blocks_of(2 * T)

    ins = (first_ref, feed_ref)
    ws = (wa_ref, wf_ref)
    lcs, lys, lzs = (lca_ref, lcf_ref), (lya_ref, lyf_ref), (lza_ref, lzf_ref)

    def to_x():
        return dp, z * 2 + 1 - x

    def to_z(peer):
        return dp, peer * 2 + x

    def to_y(j):
        return xor(y, j) * 2 + c, tensor

    def to_c():
        return y * 2 + 1 - c, tensor

    def remote(src, dst, send, recv, device):
        return pltpu.make_async_remote_copy(
            src_ref=src, dst_ref=dst, send_sem=send, recv_sem=recv,
            device_id=device, device_id_type=pl.DeviceIdType.MESH,
        )

    def zcopies(lane, k):
        low = k & -k
        rest = k ^ low
        there = ws[lane].at[xor(z, rest), c, y]
        source = ins[lane] if rest == 0 else there
        return [remote(source, there, zs.at[lane, k], zr.at[lane, k], to_z(xor(z, low)))]

    def ycopies(lane, k, j):
        there = ws[lane].at[xor(z, k), c, y]
        return [remote(ins[lane] if k == 0 else there, there, ys.at[lane, k, j], yr.at[lane, k, j], to_y(j))]

    def ccopy(lane, k, j):
        there = ws[lane].at[xor(z, k), c, xor(y, j)]
        own = k == 0 and j == 0
        return remote(ins[lane] if own else there, there, cs.at[lane, k, j], cr.at[lane, k, j], to_c())

    def zpass(lane, k):
        if k:
            for copy in zcopies(lane, k):
                copy.wait_recv()
            for child in children(k, NZ):
                for copy in zcopies(lane, child):
                    copy.start()
        for j in range(1, NY):
            for copy in ycopies(lane, k, j):
                copy.start()
        ccopy(lane, k, 0).start()

    def ypass(lane, k):
        for j in range(1, NY):
            for copy in ycopies(lane, k, j):
                copy.wait_recv()
            ccopy(lane, k, j).start()

    def cpass(lane, k):
        for j in range(NY):
            ccopy(lane, k, j).wait_recv()

    def sent(lane, k):
        for child in children(k, NZ):
            for copy in zcopies(lane, child):
                copy.wait_send()
        for j in range(NY):
            if j:
                for copy in ycopies(lane, k, j):
                    copy.wait_send()
            ccopy(lane, k, j).wait_send()

    def rccopy(lane, k):
        t = xor(z, k)
        return remote(ws[lane].at[t, 1 - c], lcs[lane].at[t], rcs.at[lane, k], rcr.at[lane, k], to_c())

    def rycopy(lane, k, j):
        t = xor(z, k)
        return remote(
            ws[lane].at[t, c, xor(y, j)], lys[lane].at[k, j - 1], rys.at[lane, k, j], ryr.at[lane, k, j], to_y(j)
        )

    def rzcopy(lane, k):
        low = k & -k
        return remote(
            ws[lane].at[xor(z, k), c, y], lzs[lane].at[k - 1], rzs.at[lane, k], rzr.at[lane, k], to_z(xor(z, low))
        )

    def r0(lane, k):
        rccopy(lane, k).start()

    def r1(lane, k):
        t = xor(z, k)
        rccopy(lane, k).wait_recv()
        dw, land = ws[lane], lcs[lane]

        def one(j, carry):
            dw[t, c, j] = dw[t, c, j] + land[t, j]
            return carry

        lax.fori_loop(0, NY, one, 0)
        for j in range(1, NY):
            rycopy(lane, k, j).start()

    def r2(lane, k):
        t = xor(z, k)
        total = ws[lane][t, c, y].astype(F32)
        for j in range(1, NY):
            rycopy(lane, k, j).wait_recv()
            total = total + lys[lane][k, j - 1].astype(F32)
        for child in children(k, NZ):
            rzcopy(lane, child).wait_recv()
            total = total + lzs[lane][child - 1].astype(F32)
        if k == 0:
            (dfirst_ref, dfeed_ref)[lane][...] = total
        else:
            ws[lane][t, c, y] = total.astype(BF16)
            rzcopy(lane, k).start()

    own_rows = pl.ds(pl.multiple_of(x * T, T), T)
    other_rows = pl.ds(pl.multiple_of((1 - x) * T, T), T)
    own_ext = pl.ds(pl.multiple_of(REACH + x * T, REACH), T)

    edge_ext = pl.ds(pl.multiple_of(REACH + x * (2 * T - REACH), REACH), REACH)
    rest_ext = pl.ds(pl.multiple_of(REACH + REACH * (1 - x) + x * T, REACH), T - REACH)

    half = T // 2

    def own_half(h):
        return pl.ds(pl.multiple_of(x * T + h * half, half), half)

    def other_half(h):
        return pl.ds(pl.multiple_of((1 - x) * T + h * half, half), half)

    def rows_of(h):
        return pl.ds(h * half, half)

    def swap_half(which, h):
        return swap(sa_ref.at[rows_of(h)], ra_ref.at[rows_of(h)], which + h)

    def share(ref, which, place):
        return remote(ref.at[place], ref.at[place], xs.at[which], xr.at[which], to_x())

    def swap(send, recv, which):
        return remote(send, recv, xs.at[which], xr.at[which], to_x())

    def piece(lane, t, d, lo, hi):
        if fold == 1:
            return ws[lane][t, d % 2, d // 2, lo:hi, :]
        slab = ws[lane][t, d % 2, d // 2]
        return jnp.concatenate([slab[:, f * rows : (f + 1) * rows] for f in range(fold)], axis=0)[lo:hi]

    def wide(lane, t, lo, hi):
        return jnp.concatenate([piece(lane, t, d, lo, hi) for d in range(dps)], axis=1)

    def put(lane, t, d, upper, lower):
        cut = upper.shape[0]
        if fold == 1:
            ws[lane][t, d % 2, d // 2, :cut, :] = upper.astype(BF16)
            ws[lane][t, d % 2, d // 2, cut:, :] = lower.astype(BF16)
            return
        slab = jnp.concatenate([upper, lower], axis=0)
        high = slab.shape[0] // fold
        slab = jnp.concatenate([slab[f * high : (f + 1) * high] for f in range(fold)], axis=1)
        ws[lane][t, d % 2, d // 2] = slab.astype(BF16)

    loads = [
        pltpu.make_async_copy(x_ref, out_ref, ls.at[0]),
        pltpu.make_async_copy(cot_ref, dx_ref, ls.at[1]),
        pltpu.make_async_copy(first_ref, wa_ref.at[z, c, y], ls.at[2]),
        pltpu.make_async_copy(feed_ref, wf_ref.at[z, c, y], ls.at[3]),
        pltpu.make_async_copy(cos_in, cos_ref, ls.at[5]),
        pltpu.make_async_copy(sin_in, sin_ref, ls.at[6]),
        pltpu.make_async_copy(segq_in, segq_ref, ls.at[7]),
    ]
    x_again = pltpu.make_async_copy(x_ref, da_ref.at[pl.ds(0, T)], ls.at[4])
    for load in loads:
        load.start()
    barrier = pltpu.get_barrier_semaphore()
    peers = [to_x(), to_c()] + [to_y(j) for j in range(1, NY)] + [to_z(xor(z, k)) for k in range(1, NZ)]
    for peer in peers:
        pl.semaphore_signal(barrier, inc=1, device_id=peer, device_id_type=pl.DeviceIdType.MESH)
    pl.semaphore_wait(barrier, len(peers))

    def gycopy(j):
        return remote(gain_ref, gall_ref.at[dp], gys.at[j], gyr.at[j], to_y(j))

    def gccopy(j):
        own = gall_ref.at[xor(y, j) * 2 + c]
        return remote(gain_ref if j == 0 else own, own, gcs.at[j], gcr.at[j], to_c())

    for j in range(1, NY):
        gycopy(j).start()
    gccopy(0).start()
    for k in range(1, NZ):
        if k & (k - 1) == 0:
            zcopies(0, k)[0].start()
    zpass(0, 0)
    gall_ref[dp] = gain_ref[...]
    loads[0].wait()
    normed, _ = norm_rows(out_ref[...])
    for j in range(1, NY):
        gycopy(j).wait_recv()
        gccopy(j).start()
    for j in range(NY):
        gccopy(j).wait_recv()

    def gain_row(which):
        return jnp.concatenate([gall_ref[d, which : which + 1, :] for d in range(dps)], axis=1)

    a1_ref[own_ext, :] = (normed * gain_row(0)).astype(BF16)
    share(a1_ref, EX_EDGE, edge_ext).start()
    share(a1_ref, EX_A1, rest_ext).start()
    loads[1].wait()
    up_ref[own_rows, :] = dx_ref[...].astype(BF16)
    for load in loads[2:]:
        load.wait()
    dqkv_ref[...] = jnp.zeros_like(dqkv_ref)
    edge = jnp.zeros((REACH, D), BF16)

    @pl.when(z == 0)
    def _():
        a1_ref[:REACH, :] = edge

    @pl.when(z == NZ - 1)
    def _():
        a1_ref[ext - REACH :, :] = edge

    def halo(which, send, recv):
        peer = z - 1 if which == 0 else z + 1
        return remote(send, recv, hss.at[which], hrs.at[which], to_z(peer))

    def halo_a(which):
        if which == 0:
            return halo(0, a1_ref.at[pl.ds(REACH, REACH)], a1_ref.at[pl.ds(ext - REACH, REACH)])
        return halo(1, a1_ref.at[pl.ds(2 * T, REACH)], a1_ref.at[pl.ds(0, REACH)])

    def halo_d(which):
        peer = z - 1 if which == 0 else z + 1
        return remote(hs_ref.at[which], hr_ref.at[1 - which], hss.at[2 + which], hrs.at[2 + which], to_z(peer))

    def halo_start(maker):
        @pl.when(z > 0)
        def _():
            maker(0).start()

        @pl.when(z < NZ - 1)
        def _():
            maker(1).start()

    def halo_wait(maker):
        @pl.when(z > 0)
        def _():
            maker(1).wait_recv()

        @pl.when(z < NZ - 1)
        def _():
            maker(0).wait_recv()

    def halo_sent(maker):
        @pl.when(z > 0)
        def _():
            maker(0).wait_send()

        @pl.when(z < NZ - 1)
        def _():
            maker(1).wait_send()

    share(a1_ref, EX_EDGE, edge_ext).wait_recv()
    halo_start(halo_a)
    zpass(0, 1)
    ypass(0, 0)
    zpass(0, 2)
    for copy in zcopies(1, 1):
        copy.start()
    ypass(0, 1)
    share(a1_ref, EX_A1, rest_ext).wait_recv()
    share(up_ref, EX_UP, own_rows).start()
    halo_wait(halo_a)

    def band(start, size, span):
        row = lax.broadcasted_iota(jnp.int32, (size, span), 0)
        col = lax.broadcasted_iota(jnp.int32, (size, span), 1)
        near = jnp.abs(row + REACH - col) <= REACH
        return near & (segq_ref[start : start + size, :] == segk_ref[:, start : start + span])

    def at_tick(i, count, act):
        for tick in range(count):
            @pl.when(i == tick)
            def _(tick=tick):
                act(tick)

    def attend(i, carry):
        def control(tick):
            if tick and tick + 2 < NZ:
                zpass(0, tick + 2)
            if tick >= NZ - 2:
                zpass(1, tick + 2 - NZ)
            if tick >= 2:
                ypass(0, tick)
            if tick == min(2, NZ - 1):
                for k in range(2, NZ):
                    if k & (k - 1) == 0:
                        for copy in zcopies(1, k):
                            copy.start()
            cpass(0, tick)

        at_tick(i, NZ, control)
        t = xor_dynamic(z, i, NZ)
        qkv = mm(a1_ref[...], wide(0, t, 0, 3 * hw), NT)
        cos, sin = cos_ref[...], sin_ref[...]
        q, k, v = qkv[:, :hw], qkv[:, hw : 2 * hw], qkv[:, 2 * hw :].astype(BF16)
        q = (q * cos + turn(q, -1) * sin).astype(BF16)
        k = (k * cos + turn(k, -1) * sin).astype(BF16)
        qkv_ref[i, 0], qkv_ref[i, 1], qkv_ref[i, 2] = q, k, v
        for b, (start, size, span) in enumerate(blocks):
            valid = band(start, size, span)
            contexts = []
            for head in range(heads):
                lanes = slice(head * HD, (head + 1) * HD)
                qb = q[REACH + start : REACH + start + size, lanes]
                kb = k[start : start + span, lanes]
                vb = v[start : start + span, lanes]
                s = jnp.where(valid, mm(qb, kb, NT) * scale, MASKED)
                e = jnp.exp(s - jnp.max(s, axis=-1, keepdims=True))
                weights = (e * (1.0 / jnp.sum(e, axis=-1, keepdims=True))).astype(BF16)
                p_ref[i, b, head] = weights
                contexts.append(mm(weights, vb, NN))
            ctx_ref[i, start : start + size, :] = jnp.concatenate(contexts, axis=1).astype(BF16)
        return carry

    lax.fori_loop(0, NZ, attend, 0)

    def project(place):
        total = 0.0
        for i in range(NZ):
            total = total + mm(ctx_ref[i, place, :], wide(0, xor(z, i), 3 * hw, 4 * hw), NN)
        return total

    for h in range(2):
        sa_ref[rows_of(h), :] = project(other_half(h)).astype(BF16)
        swap_half(EX_Y, h).start()
    out_ref[...] += project(own_rows)
    ypass(1, 0)
    zpass(1, 2)
    for h in range(2):
        swap_half(EX_Y, h).wait()
        out_ref[rows_of(h), :] += ra_ref[rows_of(h), :].astype(F32)
        normed, _ = norm_rows(out_ref[rows_of(h), :])
        a2_ref[own_half(h), :] = (normed * gain_row(1)).astype(BF16)
        share(a2_ref, EX_A2 + h, own_half(h)).start()
    share(up_ref, EX_UP, own_rows).wait_recv()
    acc = acc_ref.at[pl.ds(0, 2 * T)]
    acc[...] = jnp.zeros((2 * T, D), F32)
    da_ref[...] = jnp.zeros_like(da_ref)

    HALF, GRAD = 0, 1
    OWN, OTHER = 0, 1
    steps = [(HALF, 0, OWN), (HALF, 1, OWN), (HALF, 0, OTHER), (GRAD, 0, 0), (HALF, 1, OTHER)]
    for k in range(2, NZ):
        steps += [(HALF, k, OTHER), (HALF, k, OWN)]
    steps += [(GRAD, k, 0) for k in range(NZ - 1, 0, -1)]

    def table(step, column):
        out = 0
        for at, row in enumerate(steps):
            if row[column]:
                out = out + row[column] * (step == at).astype(jnp.int32)
        return out

    def before(at):
        kind, k, side = steps[at]
        if kind == GRAD:
            sent(1, k)
            return
        if (k, side) == (1, OWN):
            ypass(1, 1)
            zpass(1, 3)
        if (k, side) == (0, OTHER):
            for h in range(2):
                share(a2_ref, EX_A2 + h, own_half(h)).wait_recv()
        if (k, side) == (1, OTHER):
            ypass(1, 2)
        if k >= 2 and side == OTHER:
            if k + 2 < NZ:
                zpass(1, k + 2)
            if k > 2:
                ypass(1, k)
            cpass(1, k)
        if k < 2 and side == OWN:
            cpass(1, k)

    def after(at):
        kind, k, side = steps[at]
        if kind == GRAD:
            r0(1, k)
            if 0 < k < NZ - 1:
                r1(1, k + 1)
        elif (k, side) == (2, OTHER):
            r1(1, 0)
        elif (k, side) == (NZ - 1, OTHER):
            sa_ref[...] = da_ref[other_rows, :].astype(BF16)
            for h in range(2):
                swap_half(EX_DA, h).start()

    def feed(step, carry):
        at_tick(step, len(steps), before)
        k = table(step, 1)
        t = xor_dynamic(z, k, NZ)
        kind = table(step, 0)

        @pl.when(kind == HALF)
        def _():
            side = table(step, 2)
            place = pl.ds(pl.multiple_of((x + side - 2 * x * side) * T, T), T)
            a, up = a2_ref[place, :], up_ref[place, :]
            u01 = mm(wide(1, t, 0, 2 * UP), a, NT)
            dg = mm(wide(1, t, 2 * UP, 3 * UP), up, NT)
            u0, u1 = u01[:UP], u01[UP:]
            cdf = 0.5 * (1.0 + lax.erf(u0 * ROOT_HALF))
            activated = u0 * cdf
            slope = cdf + u0 * DENSITY * jnp.exp(-0.5 * u0 * u0)
            hidden = (activated * u1).astype(BF16)
            du = jnp.concatenate([dg * u1 * slope, dg * activated], axis=0).astype(BF16)
            hd_ref[k, side, : 2 * UP, :] = du
            hd_ref[k, side, 2 * UP :, :] = hidden
            hidden_t, du_t = hidden.T, du.T
            for d in range(dps):
                cols = slice(d * rows, (d + 1) * rows)
                da_ref[place, cols] += mm(du_t, piece(1, t, d, 0, 2 * UP), NN)
                acc[place, cols] += mm(hidden_t, piece(1, t, d, 2 * UP, 3 * UP), NN)

        @pl.when(kind == GRAD)
        def _():
            mine, theirs = hd_ref[k, 0], hd_ref[k, 1]
            for d in range(dps):
                cols = slice(d * rows, (d + 1) * rows)
                upper = mm(mine[: 2 * UP], a2_ref[own_rows, cols], NN)
                upper = upper + mm(theirs[: 2 * UP], a2_ref[other_rows, cols], NN)
                lower = mm(mine[2 * UP :], up_ref[own_rows, cols], NN)
                lower = lower + mm(theirs[2 * UP :], up_ref[other_rows, cols], NN)
                put(1, t, d, upper, lower)

        at_tick(step, len(steps), after)
        return carry

    lax.fori_loop(0, len(steps), feed, 0)

    sb_ref[...] = acc[other_rows, :].astype(BF16)
    gain_two = jnp.zeros((1, D), F32)
    for h in range(2):
        swap_half(EX_DA, h).wait()
        da_own = da_ref[own_half(h), :] + ra_ref[rows_of(h), :].astype(F32)
        normed, inverse = norm_rows(out_ref[rows_of(h), :])
        dx_ref[rows_of(h), :] += norm_back(da_own, normed, inverse, gain_row(1))
        dy_ref[own_half(h), :] = dx_ref[rows_of(h), :].astype(BF16)
        share(dy_ref, EX_DY + h, own_half(h)).start()
        gain_two = gain_two + jnp.sum(da_own * normed, axis=0, keepdims=True)
    r1(1, 1)
    x_again.start()
    out_ref[...] += acc[own_rows, :]
    acc_ref[...] = jnp.zeros_like(acc_ref)
    r2(1, NZ - 1)
    for h in range(2):
        share(dy_ref, EX_DY + h, own_half(h)).wait_recv()
    swap(sb_ref, rb_ref, EX_OUT).start()

    inner = slice(REACH, REACH + 2 * T)

    def attend_back(step, carry):
        i = NZ - 1 - step
        t = xor_dynamic(z, i, NZ)
        dyb = dy_ref[...]
        dc = mm(dyb, wide(0, t, 3 * hw, 4 * hw), NT).astype(BF16)
        dk_ref[...] = jnp.zeros_like(dk_ref)
        dv_ref[...] = jnp.zeros_like(dv_ref)
        dq_rows = []
        for b, (start, size, span) in enumerate(blocks):
            dq_parts, dk_parts, dv_parts = [], [], []
            for head in range(heads):
                lanes = slice(head * HD, (head + 1) * HD)
                qb = qkv_ref[i, 0, REACH + start : REACH + start + size, lanes]
                kb = qkv_ref[i, 1, start : start + span, lanes]
                vb = qkv_ref[i, 2, start : start + span, lanes]
                db = dc[start : start + size, lanes]
                weights = p_ref[i, b, head]
                probs = weights.astype(F32)
                dpr = mm(db, vb, NT)
                delta = jnp.sum(probs * dpr, axis=-1, keepdims=True)
                ds = (probs * (dpr - delta) * scale).astype(BF16)
                dq_parts.append(mm(ds, kb, NN))
                dk_parts.append(mm(ds, qb, TN))
                dv_parts.append(mm(weights, db, TN))
            dq_rows.append(jnp.concatenate(dq_parts, axis=1))
            dk_ref[start : start + span, :] += jnp.concatenate(dk_parts, axis=1)
            dv_ref[start : start + span, :] += jnp.concatenate(dv_parts, axis=1)
        cos, sin = cos_ref[...], sin_ref[...]
        dq = jnp.concatenate(dq_rows, axis=0)
        dk = dk_ref[...]
        dqkv_ref[inner, :hw] = (dq * cos[inner] + turn(dq * sin[inner], 1)).astype(BF16)
        dqkv_ref[:, hw : 2 * hw] = (dk * cos + turn(dk * sin, 1)).astype(BF16)
        dqkv_ref[:, 2 * hw :] = dv_ref[...].astype(BF16)
        acc_ref[...] += mm(dqkv_ref[...], wide(0, t, 0, 3 * hw), NN)
        dqkv_t, ctx_t = dqkv_ref[...].T, ctx_ref[i].T
        for d in range(dps):
            cols = slice(d * rows, (d + 1) * rows)
            put(0, t, d, mm(dqkv_t, a1_ref[:, cols], NN), mm(ctx_t, dy_ref[:, cols], NN))

        def control(tick):
            k = NZ - 1 - tick
            r0(0, k)
            if k + 1 < NZ:
                r1(0, k + 1)
            if tick == 1:
                r2(1, NZ - 2)
            if tick == 3:
                r2(1, NZ - 3)

        at_tick(step, NZ, control)
        return carry

    for k in range(NZ):
        sent(0, k)
    lax.fori_loop(0, NZ, attend_back, 0)

    hs_ref[0] = acc_ref[:REACH, :].astype(BF16)
    hs_ref[1] = acc_ref[ext - REACH :, :].astype(BF16)
    halo_start(halo_d)
    swap(sb_ref, rb_ref, EX_OUT).wait()
    out_ref[...] += rb_ref[...].astype(F32)
    bulk = pl.ds(pl.multiple_of(REACH + REACH * x + (1 - x) * T, REACH), T - REACH)
    sa_ref[: T - REACH, :] = acc_ref[bulk, :].astype(BF16)
    bulk_out = swap(sa_ref.at[pl.ds(0, T - REACH)], ra_ref.at[pl.ds(0, T - REACH)], EX_DX)
    bulk_out.start()
    gain_one = jnp.sum(acc_ref[...] * a1_ref[...].astype(F32), axis=0, keepdims=True) / gain_row(0)
    for d in range(dps):
        cols = slice(d * rows, (d + 1) * rows)
        gsum_ref[d] = jnp.concatenate(
            [gain_one[:, cols], gain_two[:, cols], jnp.zeros((6, rows), F32)], axis=0
        )
    stages = [to_c()]
    stages += [to_y(2**b) for b in range(NY.bit_length() - 1)]
    stages += [to_z(xor(z, 2**b)) for b in range(NZ.bit_length() - 1)] + [to_x()]

    def gcopy(s):
        return remote(gsum_ref, gland_ref.at[s], gss.at[s], gsr.at[s], stages[s])

    def gain_stage(s):
        gcopy(s).wait()
        gsum_ref[...] += gland_ref[s]
        if s + 1 < len(stages):
            gcopy(s + 1).start()

    gcopy(0).start()
    gain_stage(0)
    r1(0, 0)
    halo_wait(halo_d)

    @pl.when(z > 0)
    def _():
        acc_ref[REACH : 2 * REACH, :] += hr_ref[0].astype(F32)

    @pl.when(z < NZ - 1)
    def _():
        acc_ref[ext - 2 * REACH : ext - REACH, :] += hr_ref[1].astype(F32)

    far_edge = pl.ds(pl.multiple_of(REACH + (1 - x) * (2 * T - REACH), REACH), REACH)
    es_ref[...] = acc_ref[far_edge, :].astype(BF16)
    swap(es_ref, er_ref, EX_DEDGE).start()
    gain_stage(1)
    r2(0, NZ - 1)
    gain_stage(2)
    for k in range(NZ - 2, 1, -1):
        r2(0, k)
    gain_stage(3)
    x_again.wait()
    normed, inverse = norm_rows(da_ref[:T, :])
    bulk_out.wait()
    swap(es_ref, er_ref, EX_DEDGE).wait()
    acc_ref[rest_ext, :] += ra_ref[: T - REACH, :].astype(F32)
    acc_ref[edge_ext, :] += er_ref[...].astype(F32)
    dx_ref[...] += norm_back(acc_ref[own_ext, :], normed, inverse, gain_row(0))
    r2(0, 1)
    for s in range(4, len(stages)):
        gain_stage(s)
    gg_ref[...] = gsum_ref[dp]
    for k in range(NZ - 4, 0, -1):
        r2(1, k)
    r2(1, 0)
    r2(0, 0)

    for j in range(1, NY):
        gycopy(j).wait_send()
    for j in range(NY):
        gccopy(j).wait_send()
    for lane in range(2):
        for k in range(NZ):
            if k:
                rzcopy(lane, k).wait_send()
            for j in range(1, NY):
                rycopy(lane, k, j).wait_send()
            rccopy(lane, k).wait_send()
    share(a1_ref, EX_EDGE, edge_ext).wait_send()
    share(a1_ref, EX_A1, rest_ext).wait_send()
    share(up_ref, EX_UP, own_rows).wait_send()
    for h in range(2):
        share(a2_ref, EX_A2 + h, own_half(h)).wait_send()
        share(dy_ref, EX_DY + h, own_half(h)).wait_send()
    halo_sent(halo_a)
    halo_sent(halo_d)


def body(
    dps,
    tensors,
    block_input,
    segment_ids,
    positions,
    attention_gain,
    feedforward_gain,
    qkv_weight,
    output_weight,
    expand_weight,
    contract_weight,
    cotangent,
):
    T, D = block_input.shape[1:]
    rows = qkv_weight.shape[0]
    hw = qkv_weight.shape[2]
    units = contract_weight.shape[0]
    fold = max(1, 128 // rows)
    UP = -(-units // (8 * fold)) * 8 * fold
    heads = hw // HD
    ext = 2 * T + 2 * REACH
    NY, NZ = dps // 2, tensors // 2

    pair = lax.axis_index("tensor") // 2
    seg_all = jnp.pad(segment_ids[0], (REACH, REACH), constant_values=-1)
    pos_all = jnp.pad(positions[0], (REACH, REACH))
    seg_k = lax.dynamic_slice_in_dim(seg_all, pair * 2 * T, ext, 0)
    pos = lax.dynamic_slice_in_dim(pos_all, pair * 2 * T, ext, 0)
    seg_q = seg_k[REACH : REACH + 2 * T]
    half = HD // 2
    frequency = jnp.exp(jnp.arange(half, dtype=F32) * (-2.0 * math.log(10000.0) / HD))
    angles = pos.astype(F32)[:, None] * frequency[None, :]
    cos = jnp.tile(jnp.cos(angles), (1, 2 * heads))
    sin = jnp.tile(jnp.sin(angles), (1, 2 * heads))

    gains = jnp.pad(jnp.stack([attention_gain, feedforward_gain]).astype(F32), ((0, 6), (0, 0)))
    first = jnp.concatenate(
        [jnp.transpose(qkv_weight, (1, 2, 0)).reshape(3 * hw, rows), output_weight], axis=0
    )
    stacked = jnp.concatenate([jnp.transpose(expand_weight, (1, 2, 0)), contract_weight[None]], axis=0)
    stacked = jnp.pad(stacked, ((0, 0), (0, UP - units), (0, 0))).reshape(3 * UP, rows)

    def folded(slab):
        high = slab.shape[0] // fold
        return jnp.concatenate([slab[f * high : (f + 1) * high] for f in range(fold)], axis=1)

    def unfolded(slab):
        return jnp.concatenate([slab[:, f * rows : (f + 1) * rows] for f in range(fold)], axis=0)

    if fold > 1:
        first, stacked = folded(first), folded(stacked)
    blocks = blocks_of(2 * T)
    size, span = blocks[0][1:]
    n_stage = 2 + (NY.bit_length() - 1) + (NZ.bit_length() - 1)
    vm, dma = pltpu.VMEM, pltpu.SemaphoreType.DMA
    fa, ff = first.shape, stacked.shape
    ny1, nz1 = max(NY - 1, 1), max(NZ - 1, 1)
    scratch = [
        vm((ext, hw), F32), vm((ext, hw), F32), vm((2 * T, 1), jnp.int32),
        vm((NZ, 2, NY) + fa, BF16), vm((NZ, 2, NY) + ff, BF16), vm((NZ, 2, 3 * UP, T), BF16),
        vm((NZ, NY) + fa, BF16), vm((NZ, NY) + ff, BF16),
        vm((NZ, ny1) + fa, BF16), vm((NZ, ny1) + ff, BF16),
        vm((nz1,) + fa, BF16), vm((nz1,) + ff, BF16),
        vm((dps, 8, rows), F32), vm((dps, 8, rows), F32), vm((n_stage, dps, 8, rows), F32),
        vm((ext, D), BF16), vm((2 * T, D), BF16), vm((2 * T, D), BF16), vm((2 * T, D), BF16),
        vm((ext, D), F32), vm((2 * T, D), F32),
        vm((NZ, 3, ext, hw), BF16), vm((NZ, 2 * T, hw), BF16),
        vm((NZ, len(blocks), heads, size, span), BF16),
        vm((ext, hw), F32), vm((ext, hw), F32), vm((ext, 3 * hw), BF16),
        vm((T, D), BF16), vm((T, D), BF16), vm((T, D), BF16), vm((T, D), BF16),
        vm((2, REACH, D), BF16), vm((2, REACH, D), BF16), vm((REACH, D), BF16), vm((REACH, D), BF16),
        dma((2, NZ)), dma((2, NZ)), dma((2, NZ, NY)), dma((2, NZ, NY)), dma((2, NZ, NY)), dma((2, NZ, NY)),
        dma((2, NZ)), dma((2, NZ)), dma((2, NZ, NY)), dma((2, NZ, NY)), dma((2, NZ)), dma((2, NZ)),
        dma((14,)), dma((14,)), dma((4,)), dma((4,)),
        dma((NY,)), dma((NY,)), dma((NY,)), dma((NY,)), dma((n_stage,)), dma((n_stage,)), dma((8,)),
    ]
    out, dx, gg, dfirst, dfeed = pl.pallas_call(
        functools.partial(layer_kernel, dps, tensors, units),
        in_specs=[
            pl.BlockSpec(memory_space=pl.ANY if i in (0, 1, 3, 4, 5, 6, 7) else pltpu.VMEM) for i in range(9)
        ],
        out_specs=[pl.BlockSpec(memory_space=pltpu.VMEM)] * 5,
        out_shape=[
            jax.ShapeDtypeStruct((T, D), F32),
            jax.ShapeDtypeStruct((T, D), F32),
            jax.ShapeDtypeStruct((8, rows), F32),
            jax.ShapeDtypeStruct(fa, F32),
            jax.ShapeDtypeStruct(ff, F32),
        ],
        scratch_shapes=scratch,
        compiler_params=pltpu.CompilerParams(
            collective_id=0, has_side_effects=True, vmem_limit_bytes=63 * 1024 * 1024
        ),
        name="layer",
    )(block_input[0], cotangent[0], gains, first, stacked, cos, sin, seg_q[:, None], seg_k[None, :])

    if fold > 1:
        dfirst, dfeed = unfolded(dfirst), unfolded(dfeed)
    dqkv = dfirst[: 3 * hw].reshape(3, hw, rows)
    dfeed = dfeed.reshape(3, UP, rows)[:, :units]
    return (
        out[None],
        dx[None],
        gg[0],
        gg[1],
        jnp.transpose(dqkv, (2, 0, 1)),
        dfirst[3 * hw :],
        jnp.transpose(dfeed[:2], (2, 0, 1)),
        dfeed[2],
    )


def solution(mesh):
    return jax.shard_map(
        functools.partial(body, mesh.shape["dp"], mesh.shape["tensor"]),
        mesh=mesh,
        in_specs=(
            P("dp", "tensor", None),
            P("dp", None),
            P("dp", None),
            P("dp"),
            P("dp"),
            P("dp", None, "tensor"),
            P("tensor", "dp"),
            P("dp", None, "tensor"),
            P("tensor", "dp"),
            P("dp", "tensor", None),
        ),
        out_specs=(
            P("dp", "tensor", None),
            P("dp", "tensor", None),
            P("dp"),
            P("dp"),
            P("dp", None, "tensor"),
            P("tensor", "dp"),
            P("dp", None, "tensor"),
            P("tensor", "dp"),
        ),
        check_vma=False,
    )
```

```python
import functools
import math

import jax
import jax.numpy as jnp
from jax import lax
from jax.experimental import pallas as pl
from jax.experimental.pallas import tpu as pltpu
from jax.sharding import PartitionSpec as P

HD = 64
WINDOW = 128
REACH = WINDOW // 2
EPSILON = 1e-05
MASKED = -1e30
ROOT_HALF = 0.7071067811865476
DENSITY = 0.3989422804014327
NN = (((1,), (0,)), ((), ()))
NT = (((1,), (1,)), ((), ()))
TN = (((0,), (0,)), ((), ()))
F32, BF16 = jnp.float32, jnp.bfloat16
EX_A1, EX_UP, EX_OUT, EX_DX, EX_EDGE, EX_DEDGE = range(6)
EX_Y, EX_A2, EX_DA, EX_DY = 6, 8, 10, 12


def mm(left, right, dims):
    return lax.dot_general(left, right, dims, preferred_element_type=F32)


def norm_rows(values):
    centre = values - jnp.mean(values, axis=-1, keepdims=True)
    variance = jnp.mean(centre * centre, axis=-1, keepdims=True)
    inverse = lax.rsqrt(variance + EPSILON)
    return centre * inverse, inverse


def norm_back(upstream, normed, inverse, gain):
    scaled = upstream * gain
    inner = (
        scaled
        - jnp.mean(scaled, axis=-1, keepdims=True)
        - normed * jnp.mean(scaled * normed, axis=-1, keepdims=True)
    )
    return inverse * inner


def xor(value, k):
    bit, out = 1, value
    while bit <= k:
        if k & bit:
            out = out + bit * (1 - 2 * ((value // bit) % 2))
        bit *= 2
    return out


def xor_dynamic(value, k, count):
    bit, out = 1, 0
    while bit < count:
        out = out + bit * (((value // bit) + (k // bit)) % 2)
        bit *= 2
    return out


def children(k, count):
    low = (k & -k) if k else count
    bit, found = 1, []
    while bit < low:
        found.append(k + bit)
        bit *= 2
    return found


def turn(tensor, first_sign):
    half = HD // 2
    pieces = []
    for head in range(tensor.shape[1] // HD):
        low = tensor[:, head * HD : head * HD + half]
        high = tensor[:, head * HD + half : (head + 1) * HD]
        pieces += [-high, low] if first_sign < 0 else [high, -low]
    return jnp.concatenate(pieces, axis=1)


def blocks_of(tokens):
    size = min(tokens, 128)
    return [(start, size, size + 2 * REACH) for start in range(0, tokens, size)]


def layer_kernel(
    dps, tensors, units,
    x_ref, cot_ref, gain_ref, first_ref, feed_ref, cos_in, sin_in, segq_in, segk_ref,
    out_ref, dx_ref, g1_ref, g2_ref, dqkv_out, dproj_out, dup_out, ddown_out,
    cos_ref, sin_ref, segq_ref, wa_ref, wf_ref, hd_ref,
    lca_ref, lcf_ref, lya_ref, lyf_ref, lza_ref, lzf_ref, lzq_ref,
    gall_ref, gsum_ref, gland_ref,
    a1_ref, a2_ref, up_ref, dy_ref, acc_ref, da_ref,
    qkv_ref, ctx_ref, p_ref, dk_ref, dv_ref, dqkv_ref,
    sa_ref, ra_ref, sb_ref, rb_ref, hs_ref, hr_ref, es_ref, er_ref,
    zs, zr, ys, yr, cs, cr,
    rcs, rcr, rys, ryr, rzs, rzr,
    xs, xr, hss, hrs, gys, gyr, gcs, gcr, gss, gsr, ls,
):
    NY, NZ = dps // 2, tensors // 2
    dp, tensor = lax.axis_index("dp"), lax.axis_index("tensor")
    y, c = dp // 2, dp % 2
    z, x = tensor // 2, tensor % 2
    T, D = x_ref.shape
    rows = D // dps
    fold = first_ref.shape[1] // rows
    hw = first_ref.shape[0] * fold // 4
    UP = feed_ref.shape[0] * fold // 3
    heads = hw // HD
    ext = 2 * T + 2 * REACH
    scale = HD ** (-0.5)
    blocks = blocks_of(2 * T)

    ins = (first_ref, feed_ref)
    ws = (wa_ref, wf_ref)
    lcs, lys, lzs = (lca_ref, lcf_ref), (lya_ref, lyf_ref), (lza_ref, lzf_ref)

    def to_x():
        return dp, z * 2 + 1 - x

    def to_z(peer):
        return dp, peer * 2 + x

    def to_y(j):
        return xor(y, j) * 2 + c, tensor

    def to_c():
        return y * 2 + 1 - c, tensor

    def remote(src, dst, send, recv, device):
        return pltpu.make_async_remote_copy(
            src_ref=src, dst_ref=dst, send_sem=send, recv_sem=recv,
            device_id=device, device_id_type=pl.DeviceIdType.MESH,
        )

    def zcopies(lane, k):
        low = k & -k
        rest = k ^ low
        there = ws[lane].at[xor(z, rest), c, y]
        source = ins[lane] if rest == 0 else there
        return [remote(source, there, zs.at[lane, k], zr.at[lane, k], to_z(xor(z, low)))]

    def ycopies(lane, k, j):
        there = ws[lane].at[xor(z, k), c, y]
        return [remote(ins[lane] if k == 0 else there, there, ys.at[lane, k, j], yr.at[lane, k, j], to_y(j))]

    def ccopy(lane, k, j):
        there = ws[lane].at[xor(z, k), c, xor(y, j)]
        own = k == 0 and j == 0
        return remote(ins[lane] if own else there, there, cs.at[lane, k, j], cr.at[lane, k, j], to_c())

    def zpass(lane, k):
        if k:
            for copy in zcopies(lane, k):
                copy.wait_recv()
            for child in children(k, NZ):
                for copy in zcopies(lane, child):
                    copy.start()
        for j in range(1, NY):
            for copy in ycopies(lane, k, j):
                copy.start()
        ccopy(lane, k, 0).start()

    def ypass(lane, k):
        for j in range(1, NY):
            for copy in ycopies(lane, k, j):
                copy.wait_recv()
            ccopy(lane, k, j).start()

    def cpass(lane, k):
        for j in range(NY):
            ccopy(lane, k, j).wait_recv()

    def sent(lane, k):
        for child in children(k, NZ):
            for copy in zcopies(lane, child):
                copy.wait_send()
        for j in range(NY):
            if j:
                for copy in ycopies(lane, k, j):
                    copy.wait_send()
            ccopy(lane, k, j).wait_send()

    def rccopy(lane, k):
        t = xor(z, k)
        return remote(ws[lane].at[t, 1 - c], lcs[lane].at[t], rcs.at[lane, k], rcr.at[lane, k], to_c())

    def rycopy(lane, k, j):
        t = xor(z, k)
        return remote(
            ws[lane].at[t, c, xor(y, j)], lys[lane].at[k, j - 1], rys.at[lane, k, j], ryr.at[lane, k, j], to_y(j)
        )

    def rzcopy(lane, k):
        low = k & -k
        return remote(
            ws[lane].at[xor(z, k), c, y], lzs[lane].at[k - 1], rzs.at[lane, k], rzr.at[lane, k], to_z(xor(z, low))
        )

    def rqcopy():
        return remote(ws[1].at[xor(z, 1), c], lzq_ref, rzs.at[1, 1], rzr.at[1, 1], to_z(xor(z, 1)))

    def r0(lane, k):
        rccopy(lane, k).start()

    def r1(lane, k):
        t = xor(z, k)
        rccopy(lane, k).wait_recv()
        dw, land = ws[lane], lcs[lane]

        def one(j, carry):
            dw[t, c, j] = dw[t, c, j] + land[t, j]
            return carry

        lax.fori_loop(0, NY, one, 0)
        if (lane, k) == (1, 1):
            rqcopy().start()
            return
        if (lane, k) == (1, 0):
            rqcopy().wait_recv()

            def more(j, carry):
                dw[t, c, j] = dw[t, c, j] + lzq_ref[j]
                return carry

            lax.fori_loop(0, NY, more, 0)
        for j in range(1, NY):
            rycopy(lane, k, j).start()

    def r2(lane, k):
        if (lane, k) == (1, 1):
            return
        t = xor(z, k)
        total = ws[lane][t, c, y].astype(F32)
        for j in range(1, NY):
            rycopy(lane, k, j).wait_recv()
            total = total + lys[lane][k, j - 1].astype(F32)
        for child in children(k, NZ):
            if (lane, child) == (1, 1):
                continue
            rzcopy(lane, child).wait_recv()
            total = total + lzs[lane][child - 1].astype(F32)
        if k == 0:
            upper, lower = ((dqkv_out, dproj_out), (dup_out, ddown_out))[lane]
            if fold > 1:
                total = jnp.concatenate([total[:, f * rows : (f + 1) * rows] for f in range(fold)], axis=0)
            cut = upper.shape[0]
            upper[...], lower[...] = total[:cut], total[cut:]
        else:
            ws[lane][t, c, y] = total.astype(BF16)
            rzcopy(lane, k).start()

    own_rows = pl.ds(pl.multiple_of(x * T, T), T)
    other_rows = pl.ds(pl.multiple_of((1 - x) * T, T), T)
    own_ext = pl.ds(pl.multiple_of(REACH + x * T, REACH), T)

    edge_ext = pl.ds(pl.multiple_of(REACH + x * (2 * T - REACH), REACH), REACH)
    rest_ext = pl.ds(pl.multiple_of(REACH + REACH * (1 - x) + x * T, REACH), T - REACH)

    half = T // 2

    def own_half(h):
        return pl.ds(pl.multiple_of(x * T + h * half, half), half)

    def other_half(h):
        return pl.ds(pl.multiple_of((1 - x) * T + h * half, half), half)

    def rows_of(h):
        return pl.ds(h * half, half)

    def swap_half(which, h):
        return swap(sa_ref.at[rows_of(h)], ra_ref.at[rows_of(h)], which + h)

    def share(ref, which, place):
        return remote(ref.at[place], ref.at[place], xs.at[which], xr.at[which], to_x())

    def swap(send, recv, which):
        return remote(send, recv, xs.at[which], xr.at[which], to_x())

    def piece(lane, t, d, lo, hi):
        if fold == 1:
            return ws[lane][t, d % 2, d // 2, lo:hi, :]
        slab = ws[lane][t, d % 2, d // 2]
        return jnp.concatenate([slab[:, f * rows : (f + 1) * rows] for f in range(fold)], axis=0)[lo:hi]

    def wide(lane, t, lo, hi):
        return jnp.concatenate([piece(lane, t, d, lo, hi) for d in range(dps)], axis=1)

    def put(lane, t, d, upper, lower):
        cut = upper.shape[0]
        if fold == 1:
            ws[lane][t, d % 2, d // 2, :cut, :] = upper.astype(BF16)
            ws[lane][t, d % 2, d // 2, cut:, :] = lower.astype(BF16)
            return
        slab = jnp.concatenate([upper, lower], axis=0)
        high = slab.shape[0] // fold
        slab = jnp.concatenate([slab[f * high : (f + 1) * high] for f in range(fold)], axis=1)
        ws[lane][t, d % 2, d // 2] = slab.astype(BF16)

    loads = [
        pltpu.make_async_copy(x_ref, out_ref, ls.at[0]),
        pltpu.make_async_copy(cot_ref, dx_ref, ls.at[1]),
        pltpu.make_async_copy(first_ref, wa_ref.at[z, c, y], ls.at[2]),
        pltpu.make_async_copy(feed_ref, wf_ref.at[z, c, y], ls.at[3]),
        pltpu.make_async_copy(cos_in, cos_ref, ls.at[5]),
        pltpu.make_async_copy(sin_in, sin_ref, ls.at[6]),
        pltpu.make_async_copy(segq_in, segq_ref, ls.at[7]),
    ]
    x_again = pltpu.make_async_copy(x_ref, da_ref.at[pl.ds(0, T)], ls.at[4])
    for load in loads:
        load.start()
    barrier = pltpu.get_barrier_semaphore()
    peers = [to_x(), to_c()] + [to_y(j) for j in range(1, NY)] + [to_z(xor(z, k)) for k in range(1, NZ)]
    for peer in peers:
        pl.semaphore_signal(barrier, inc=1, device_id=peer, device_id_type=pl.DeviceIdType.MESH)
    pl.semaphore_wait(barrier, len(peers))

    def gycopy(j):
        return remote(gain_ref, gall_ref.at[dp], gys.at[j], gyr.at[j], to_y(j))

    def gccopy(j):
        own = gall_ref.at[xor(y, j) * 2 + c]
        return remote(gain_ref if j == 0 else own, own, gcs.at[j], gcr.at[j], to_c())

    for j in range(1, NY):
        gycopy(j).start()
    gccopy(0).start()
    for k in range(1, NZ):
        if k & (k - 1) == 0:
            zcopies(0, k)[0].start()
    zpass(0, 0)
    gall_ref[dp] = gain_ref[...]
    loads[0].wait()
    normed, _ = norm_rows(out_ref[...])
    for j in range(1, NY):
        gycopy(j).wait_recv()
        gccopy(j).start()
    for j in range(NY):
        gccopy(j).wait_recv()

    def gain_row(which):
        return jnp.concatenate([gall_ref[d, which : which + 1, :] for d in range(dps)], axis=1)

    a1_ref[own_ext, :] = (normed * gain_row(0)).astype(BF16)
    share(a1_ref, EX_EDGE, edge_ext).start()
    share(a1_ref, EX_A1, rest_ext).start()
    loads[1].wait()
    up_ref[own_rows, :] = dx_ref[...].astype(BF16)
    for load in loads[2:]:
        load.wait()
    dqkv_ref[...] = jnp.zeros_like(dqkv_ref)
    edge = jnp.zeros((REACH, D), BF16)

    @pl.when(z == 0)
    def _():
        a1_ref[:REACH, :] = edge

    @pl.when(z == NZ - 1)
    def _():
        a1_ref[ext - REACH :, :] = edge

    def halo(which, send, recv):
        peer = z - 1 if which == 0 else z + 1
        return remote(send, recv, hss.at[which], hrs.at[which], to_z(peer))

    def halo_a(which):
        if which == 0:
            return halo(0, a1_ref.at[pl.ds(REACH, REACH)], a1_ref.at[pl.ds(ext - REACH, REACH)])
        return halo(1, a1_ref.at[pl.ds(2 * T, REACH)], a1_ref.at[pl.ds(0, REACH)])

    def halo_d(which):
        peer = z - 1 if which == 0 else z + 1
        return remote(hs_ref.at[which], hr_ref.at[1 - which], hss.at[2 + which], hrs.at[2 + which], to_z(peer))

    def halo_start(maker):
        @pl.when(z > 0)
        def _():
            maker(0).start()

        @pl.when(z < NZ - 1)
        def _():
            maker(1).start()

    def halo_wait(maker):
        @pl.when(z > 0)
        def _():
            maker(1).wait_recv()

        @pl.when(z < NZ - 1)
        def _():
            maker(0).wait_recv()

    def halo_sent(maker):
        @pl.when(z > 0)
        def _():
            maker(0).wait_send()

        @pl.when(z < NZ - 1)
        def _():
            maker(1).wait_send()

    share(a1_ref, EX_EDGE, edge_ext).wait_recv()
    halo_start(halo_a)
    zpass(0, 1)
    ypass(0, 0)
    zpass(0, 2)
    for copy in zcopies(1, 1):
        copy.start()
    ypass(0, 1)
    share(a1_ref, EX_A1, rest_ext).wait_recv()
    share(up_ref, EX_UP, own_rows).start()
    halo_wait(halo_a)

    def band(start, size, span):
        row = lax.broadcasted_iota(jnp.int32, (size, span), 0)
        col = lax.broadcasted_iota(jnp.int32, (size, span), 1)
        near = jnp.abs(row + REACH - col) <= REACH
        return near & (segq_ref[start : start + size, :] == segk_ref[:, start : start + span])

    def at_tick(i, count, act):
        for tick in range(count):
            @pl.when(i == tick)
            def _(tick=tick):
                act(tick)

    def attend(i, carry):
        def control(tick):
            if tick and tick + 2 < NZ:
                zpass(0, tick + 2)
            if tick >= NZ - 2:
                zpass(1, tick + 2 - NZ)
            if tick >= 2:
                ypass(0, tick)
            if tick == min(2, NZ - 1):
                for k in range(2, NZ):
                    if k & (k - 1) == 0:
                        for copy in zcopies(1, k):
                            copy.start()
            cpass(0, tick)

        at_tick(i, NZ, control)
        t = xor_dynamic(z, i, NZ)
        qkv = mm(a1_ref[...], wide(0, t, 0, 3 * hw), NT)
        cos, sin = cos_ref[...], sin_ref[...]
        q, k, v = qkv[:, :hw], qkv[:, hw : 2 * hw], qkv[:, 2 * hw :].astype(BF16)
        q = (q * cos + turn(q, -1) * sin).astype(BF16)
        k = (k * cos + turn(k, -1) * sin).astype(BF16)
        qkv_ref[i, 0], qkv_ref[i, 1], qkv_ref[i, 2] = q, k, v
        for b, (start, size, span) in enumerate(blocks):
            valid = band(start, size, span)
            contexts = []
            for head in range(heads):
                lanes = slice(head * HD, (head + 1) * HD)
                qb = q[REACH + start : REACH + start + size, lanes]
                kb = k[start : start + span, lanes]
                vb = v[start : start + span, lanes]
                s = jnp.where(valid, mm(qb, kb, NT) * scale, MASKED)
                e = jnp.exp(s - jnp.max(s, axis=-1, keepdims=True))
                weights = (e * (1.0 / jnp.sum(e, axis=-1, keepdims=True))).astype(BF16)
                p_ref[i, b, head] = weights
                contexts.append(mm(weights, vb, NN))
            ctx_ref[i, start : start + size, :] = jnp.concatenate(contexts, axis=1).astype(BF16)
        return carry

    lax.fori_loop(0, NZ, attend, 0)

    def project(place):
        total = 0.0
        for i in range(NZ):
            total = total + mm(ctx_ref[i, place, :], wide(0, xor(z, i), 3 * hw, 4 * hw), NN)
        return total

    for h in range(2):
        sa_ref[rows_of(h), :] = project(other_half(h)).astype(BF16)
        swap_half(EX_Y, h).start()
    out_ref[...] += project(own_rows)
    ypass(1, 0)
    zpass(1, 2)
    for h in range(2):
        swap_half(EX_Y, h).wait()
        out_ref[rows_of(h), :] += ra_ref[rows_of(h), :].astype(F32)
        normed, _ = norm_rows(out_ref[rows_of(h), :])
        a2_ref[own_half(h), :] = (normed * gain_row(1)).astype(BF16)
        share(a2_ref, EX_A2 + h, own_half(h)).start()
    share(up_ref, EX_UP, own_rows).wait_recv()
    acc = acc_ref.at[pl.ds(0, 2 * T)]
    acc[...] = jnp.zeros((2 * T, D), F32)
    da_ref[...] = jnp.zeros_like(da_ref)

    HALF, GRAD = 0, 1
    OWN, OTHER = 0, 1
    steps = [(HALF, 0, OWN), (HALF, 1, OWN), (HALF, 0, OTHER), (HALF, 1, OTHER), (GRAD, 1, 0)]
    for k in range(2, NZ):
        steps += [(HALF, k, OTHER), (HALF, k, OWN)]
    steps += [(GRAD, k, 0) for k in list(range(NZ - 1, 1, -1)) + [0]]

    def table(step, column):
        out = 0
        for at, row in enumerate(steps):
            if row[column]:
                out = out + row[column] * (step == at).astype(jnp.int32)
        return out

    def before(at):
        kind, k, side = steps[at]
        if kind == GRAD:
            sent(1, k)
            return
        if (k, side) == (1, OWN):
            ypass(1, 1)
            zpass(1, 3)
        if (k, side) == (0, OTHER):
            for h in range(2):
                share(a2_ref, EX_A2 + h, own_half(h)).wait_recv()
        if (k, side) == (1, OTHER):
            ypass(1, 2)
        if k >= 2 and side == OTHER:
            if k + 2 < NZ:
                zpass(1, k + 2)
            if k > 2:
                ypass(1, k)
            cpass(1, k)
        if k < 2 and side == OWN:
            cpass(1, k)

    def after(at):
        kind, k, side = steps[at]
        if kind == GRAD:
            r0(1, k)
            if 1 < k < NZ - 1:
                r1(1, k + 1)
            if k == 0:
                r1(1, 2)
        elif (k, side) == (2, OTHER):
            r1(1, 1)
        elif (k, side) == (NZ - 1, OTHER):
            sa_ref[...] = da_ref[other_rows, :].astype(BF16)
            for h in range(2):
                swap_half(EX_DA, h).start()

    def feed(step, carry):
        at_tick(step, len(steps), before)
        k = table(step, 1)
        t = xor_dynamic(z, k, NZ)
        kind = table(step, 0)

        @pl.when(kind == HALF)
        def _():
            side = table(step, 2)
            place = pl.ds(pl.multiple_of((x + side - 2 * x * side) * T, T), T)
            a, up = a2_ref[place, :], up_ref[place, :]
            u01 = mm(wide(1, t, 0, 2 * UP), a, NT)
            dg = mm(wide(1, t, 2 * UP, 3 * UP), up, NT)
            u0, u1 = u01[:UP], u01[UP:]
            cdf = 0.5 * (1.0 + lax.erf(u0 * ROOT_HALF))
            activated = u0 * cdf
            slope = cdf + u0 * DENSITY * jnp.exp(-0.5 * u0 * u0)
            hidden = (activated * u1).astype(BF16)
            du = jnp.concatenate([dg * u1 * slope, dg * activated], axis=0).astype(BF16)
            hd_ref[k, side, : 2 * UP, :] = du
            hd_ref[k, side, 2 * UP :, :] = hidden
            hidden_t, du_t = hidden.T, du.T
            for d in range(dps):
                cols = slice(d * rows, (d + 1) * rows)
                da_ref[place, cols] += mm(du_t, piece(1, t, d, 0, 2 * UP), NN)
                acc[place, cols] += mm(hidden_t, piece(1, t, d, 2 * UP, 3 * UP), NN)

        @pl.when(kind == GRAD)
        def _():
            mine, theirs = hd_ref[k, 0], hd_ref[k, 1]
            for d in range(dps):
                cols = slice(d * rows, (d + 1) * rows)
                upper = mm(mine[: 2 * UP], a2_ref[own_rows, cols], NN)
                upper = upper + mm(theirs[: 2 * UP], a2_ref[other_rows, cols], NN)
                lower = mm(mine[2 * UP :], up_ref[own_rows, cols], NN)
                lower = lower + mm(theirs[2 * UP :], up_ref[other_rows, cols], NN)
                put(1, t, d, upper, lower)

        at_tick(step, len(steps), after)
        return carry

    lax.fori_loop(0, len(steps), feed, 0)

    sb_ref[...] = acc[other_rows, :].astype(BF16)
    gain_two = jnp.zeros((1, D), F32)
    for h in range(2):
        swap_half(EX_DA, h).wait()
        da_own = da_ref[own_half(h), :] + ra_ref[rows_of(h), :].astype(F32)
        normed, inverse = norm_rows(out_ref[rows_of(h), :])
        dx_ref[rows_of(h), :] += norm_back(da_own, normed, inverse, gain_row(1))
        dy_ref[own_half(h), :] = dx_ref[rows_of(h), :].astype(BF16)
        share(dy_ref, EX_DY + h, own_half(h)).start()
        gain_two = gain_two + jnp.sum(da_own * normed, axis=0, keepdims=True)
    r1(1, 0)
    x_again.start()
    out_ref[...] += acc[own_rows, :]
    acc_ref[...] = jnp.zeros_like(acc_ref)
    r2(1, NZ - 1)
    for h in range(2):
        share(dy_ref, EX_DY + h, own_half(h)).wait_recv()
    swap(sb_ref, rb_ref, EX_OUT).start()

    inner = slice(REACH, REACH + 2 * T)

    def attend_back(step, carry):
        i = NZ - 1 - step
        t = xor_dynamic(z, i, NZ)
        dyb = dy_ref[...]
        dc = mm(dyb, wide(0, t, 3 * hw, 4 * hw), NT).astype(BF16)
        dk_ref[...] = jnp.zeros_like(dk_ref)
        dv_ref[...] = jnp.zeros_like(dv_ref)
        dq_rows = []
        for b, (start, size, span) in enumerate(blocks):
            dq_parts, dk_parts, dv_parts = [], [], []
            for head in range(heads):
                lanes = slice(head * HD, (head + 1) * HD)
                qb = qkv_ref[i, 0, REACH + start : REACH + start + size, lanes]
                kb = qkv_ref[i, 1, start : start + span, lanes]
                vb = qkv_ref[i, 2, start : start + span, lanes]
                db = dc[start : start + size, lanes]
                weights = p_ref[i, b, head]
                probs = weights.astype(F32)
                dpr = mm(db, vb, NT)
                delta = jnp.sum(probs * dpr, axis=-1, keepdims=True)
                ds = (probs * (dpr - delta) * scale).astype(BF16)
                dq_parts.append(mm(ds, kb, NN))
                dk_parts.append(mm(ds, qb, TN))
                dv_parts.append(mm(weights, db, TN))
            dq_rows.append(jnp.concatenate(dq_parts, axis=1))
            dk_ref[start : start + span, :] += jnp.concatenate(dk_parts, axis=1)
            dv_ref[start : start + span, :] += jnp.concatenate(dv_parts, axis=1)
        cos, sin = cos_ref[...], sin_ref[...]
        dq = jnp.concatenate(dq_rows, axis=0)
        dk = dk_ref[...]
        dqkv_ref[inner, :hw] = (dq * cos[inner] + turn(dq * sin[inner], 1)).astype(BF16)
        dqkv_ref[:, hw : 2 * hw] = (dk * cos + turn(dk * sin, 1)).astype(BF16)
        dqkv_ref[:, 2 * hw :] = dv_ref[...].astype(BF16)
        acc_ref[...] += mm(dqkv_ref[...], wide(0, t, 0, 3 * hw), NN)
        dqkv_t, ctx_t = dqkv_ref[...].T, ctx_ref[i].T
        for d in range(dps):
            cols = slice(d * rows, (d + 1) * rows)
            put(0, t, d, mm(dqkv_t, a1_ref[:, cols], NN), mm(ctx_t, dy_ref[:, cols], NN))

        def control(tick):
            k = NZ - 1 - tick
            r0(0, k)
            if k + 1 < NZ:
                r1(0, k + 1)
            if tick == 1:
                r2(1, NZ - 2)
            if tick == 3:
                r2(1, NZ - 3)

        at_tick(step, NZ, control)
        return carry

    for k in range(NZ):
        sent(0, k)
    lax.fori_loop(0, NZ, attend_back, 0)

    hs_ref[0] = acc_ref[:REACH, :].astype(BF16)
    hs_ref[1] = acc_ref[ext - REACH :, :].astype(BF16)
    halo_start(halo_d)
    swap(sb_ref, rb_ref, EX_OUT).wait()
    out_ref[...] += rb_ref[...].astype(F32)
    bulk = pl.ds(pl.multiple_of(REACH + REACH * x + (1 - x) * T, REACH), T - REACH)
    sa_ref[: T - REACH, :] = acc_ref[bulk, :].astype(BF16)
    bulk_out = swap(sa_ref.at[pl.ds(0, T - REACH)], ra_ref.at[pl.ds(0, T - REACH)], EX_DX)
    bulk_out.start()
    gain_one = jnp.sum(acc_ref[...] * a1_ref[...].astype(F32), axis=0, keepdims=True) / gain_row(0)
    for d in range(dps):
        cols = slice(d * rows, (d + 1) * rows)
        gsum_ref[d] = jnp.concatenate(
            [gain_one[:, cols], gain_two[:, cols], jnp.zeros((6, rows), F32)], axis=0
        )
    stages = [to_c()]
    stages += [to_y(2**b) for b in range(NY.bit_length() - 1)]
    stages += [to_z(xor(z, 2**b)) for b in range(NZ.bit_length() - 1)] + [to_x()]

    def gcopy(s):
        return remote(gsum_ref, gland_ref.at[s], gss.at[s], gsr.at[s], stages[s])

    def gain_stage(s):
        gcopy(s).wait()
        gsum_ref[...] += gland_ref[s]
        if s + 1 < len(stages):
            gcopy(s + 1).start()

    gcopy(0).start()
    gain_stage(0)
    r1(0, 0)
    halo_wait(halo_d)

    @pl.when(z > 0)
    def _():
        acc_ref[REACH : 2 * REACH, :] += hr_ref[0].astype(F32)

    @pl.when(z < NZ - 1)
    def _():
        acc_ref[ext - 2 * REACH : ext - REACH, :] += hr_ref[1].astype(F32)

    far_edge = pl.ds(pl.multiple_of(REACH + (1 - x) * (2 * T - REACH), REACH), REACH)
    es_ref[...] = acc_ref[far_edge, :].astype(BF16)
    swap(es_ref, er_ref, EX_DEDGE).start()
    gain_stage(1)
    r2(0, NZ - 1)
    gain_stage(2)
    for k in range(NZ - 2, 1, -1):
        r2(0, k)
    gain_stage(3)
    x_again.wait()
    normed, inverse = norm_rows(da_ref[:T, :])
    bulk_out.wait()
    swap(es_ref, er_ref, EX_DEDGE).wait()
    acc_ref[rest_ext, :] += ra_ref[: T - REACH, :].astype(F32)
    acc_ref[edge_ext, :] += er_ref[...].astype(F32)
    dx_ref[...] += norm_back(acc_ref[own_ext, :], normed, inverse, gain_row(0))
    r2(0, 1)
    for s in range(4, len(stages)):
        gain_stage(s)
    g1_ref[...] = gsum_ref[dp, 0:1, :]
    g2_ref[...] = gsum_ref[dp, 1:2, :]
    for k in range(NZ - 4, 0, -1):
        r2(1, k)
    r2(1, 0)
    r2(0, 0)

    for j in range(1, NY):
        gycopy(j).wait_send()
    for j in range(NY):
        gccopy(j).wait_send()
    for lane in range(2):
        for k in range(NZ):
            if (lane, k) == (1, 1):
                rqcopy().wait_send()
            else:
                if k:
                    rzcopy(lane, k).wait_send()
                for j in range(1, NY):
                    rycopy(lane, k, j).wait_send()
            rccopy(lane, k).wait_send()
    share(a1_ref, EX_EDGE, edge_ext).wait_send()
    share(a1_ref, EX_A1, rest_ext).wait_send()
    share(up_ref, EX_UP, own_rows).wait_send()
    for h in range(2):
        share(a2_ref, EX_A2 + h, own_half(h)).wait_send()
        share(dy_ref, EX_DY + h, own_half(h)).wait_send()
    halo_sent(halo_a)
    halo_sent(halo_d)


def body(
    dps,
    tensors,
    block_input,
    segment_ids,
    positions,
    attention_gain,
    feedforward_gain,
    qkv_weight,
    output_weight,
    expand_weight,
    contract_weight,
    cotangent,
):
    T, D = block_input.shape[1:]
    rows = qkv_weight.shape[0]
    hw = qkv_weight.shape[2]
    units = contract_weight.shape[0]
    fold = max(1, 128 // rows)
    UP = -(-units // (8 * fold)) * 8 * fold
    heads = hw // HD
    ext = 2 * T + 2 * REACH
    NY, NZ = dps // 2, tensors // 2

    pair = lax.axis_index("tensor") // 2
    seg_all = jnp.pad(segment_ids[0], (REACH, REACH), constant_values=-1)
    pos_all = jnp.pad(positions[0], (REACH, REACH))
    seg_k = lax.dynamic_slice_in_dim(seg_all, pair * 2 * T, ext, 0)
    pos = lax.dynamic_slice_in_dim(pos_all, pair * 2 * T, ext, 0)
    seg_q = seg_k[REACH : REACH + 2 * T]
    half = HD // 2
    frequency = jnp.exp(jnp.arange(half, dtype=F32) * (-2.0 * math.log(10000.0) / HD))
    angles = pos.astype(F32)[:, None] * jnp.tile(frequency, 2 * heads)[None, :]
    cos, sin = jnp.cos(angles), jnp.sin(angles)

    gains = jnp.pad(jnp.stack([attention_gain, feedforward_gain]).astype(F32), ((0, 6), (0, 0)))
    first = jnp.concatenate(
        [jnp.transpose(qkv_weight, (1, 2, 0)).reshape(3 * hw, rows), output_weight], axis=0
    )
    stacked = jnp.concatenate([jnp.transpose(expand_weight, (1, 2, 0)), contract_weight[None]], axis=0)
    stacked = jnp.pad(stacked, ((0, 0), (0, UP - units), (0, 0))).reshape(3 * UP, rows)

    def folded(slab):
        high = slab.shape[0] // fold
        return jnp.concatenate([slab[f * high : (f + 1) * high] for f in range(fold)], axis=1)

    if fold > 1:
        first, stacked = folded(first), folded(stacked)
    blocks = blocks_of(2 * T)
    size, span = blocks[0][1:]
    n_stage = 2 + (NY.bit_length() - 1) + (NZ.bit_length() - 1)
    vm, dma = pltpu.VMEM, pltpu.SemaphoreType.DMA
    fa, ff = first.shape, stacked.shape
    ny1, nz1 = max(NY - 1, 1), max(NZ - 1, 1)
    scratch = [
        vm((ext, hw), F32), vm((ext, hw), F32), vm((2 * T, 1), jnp.int32),
        vm((NZ, 2, NY) + fa, BF16), vm((NZ, 2, NY) + ff, BF16), vm((NZ, 2, 3 * UP, T), BF16),
        vm((NZ, NY) + fa, BF16), vm((NZ, NY) + ff, BF16),
        vm((NZ, ny1) + fa, BF16), vm((NZ, ny1) + ff, BF16),
        vm((nz1,) + fa, BF16), vm((nz1,) + ff, BF16), vm((NY,) + ff, BF16),
        vm((dps, 8, rows), F32), vm((dps, 8, rows), F32), vm((n_stage, dps, 8, rows), F32),
        vm((ext, D), BF16), vm((2 * T, D), BF16), vm((2 * T, D), BF16), vm((2 * T, D), BF16),
        vm((ext, D), F32), vm((2 * T, D), F32),
        vm((NZ, 3, ext, hw), BF16), vm((NZ, 2 * T, hw), BF16),
        vm((NZ, len(blocks), heads, size, span), BF16),
        vm((ext, hw), F32), vm((ext, hw), F32), vm((ext, 3 * hw), BF16),
        vm((T, D), BF16), vm((T, D), BF16), vm((T, D), BF16), vm((T, D), BF16),
        vm((2, REACH, D), BF16), vm((2, REACH, D), BF16), vm((REACH, D), BF16), vm((REACH, D), BF16),
        dma((2, NZ)), dma((2, NZ)), dma((2, NZ, NY)), dma((2, NZ, NY)), dma((2, NZ, NY)), dma((2, NZ, NY)),
        dma((2, NZ)), dma((2, NZ)), dma((2, NZ, NY)), dma((2, NZ, NY)), dma((2, NZ)), dma((2, NZ)),
        dma((14,)), dma((14,)), dma((4,)), dma((4,)),
        dma((NY,)), dma((NY,)), dma((NY,)), dma((NY,)), dma((n_stage,)), dma((n_stage,)), dma((8,)),
    ]
    out, dx, g1, g2, dqkv, dproj, dup, ddown = pl.pallas_call(
        functools.partial(layer_kernel, dps, tensors, units),
        in_specs=[
            pl.BlockSpec(memory_space=pl.ANY if i in (0, 1, 3, 4, 5, 6, 7) else pltpu.VMEM) for i in range(9)
        ],
        out_specs=[pl.BlockSpec(memory_space=pltpu.VMEM)] * 8,
        out_shape=[
            jax.ShapeDtypeStruct((T, D), F32),
            jax.ShapeDtypeStruct((T, D), F32),
            jax.ShapeDtypeStruct((1, rows), F32),
            jax.ShapeDtypeStruct((1, rows), F32),
            jax.ShapeDtypeStruct((3 * hw, rows), F32),
            jax.ShapeDtypeStruct((hw, rows), F32),
            jax.ShapeDtypeStruct((2 * UP, rows), F32),
            jax.ShapeDtypeStruct((UP, rows), F32),
        ],
        scratch_shapes=scratch,
        compiler_params=pltpu.CompilerParams(
            collective_id=0, has_side_effects=True, vmem_limit_bytes=63 * 1024 * 1024
        ),
        name="layer",
    )(block_input[0], cotangent[0], gains, first, stacked, cos, sin, seg_q[:, None], seg_k[None, :])

    dup = dup.reshape(2, UP, rows)[:, :units]
    return (
        out[None],
        dx[None],
        g1[0],
        g2[0],
        jnp.transpose(dqkv.reshape(3, hw, rows), (2, 0, 1)),
        dproj,
        jnp.transpose(dup, (2, 0, 1)),
        ddown[:units],
    )


def solution(mesh):
    return jax.shard_map(
        functools.partial(body, mesh.shape["dp"], mesh.shape["tensor"]),
        mesh=mesh,
        in_specs=(
            P("dp", "tensor", None),
            P("dp", None),
            P("dp", None),
            P("dp"),
            P("dp"),
            P("dp", None, "tensor"),
            P("tensor", "dp"),
            P("dp", None, "tensor"),
            P("tensor", "dp"),
            P("dp", "tensor", None),
        ),
        out_specs=(
            P("dp", "tensor", None),
            P("dp", "tensor", None),
            P("dp"),
            P("dp"),
            P("dp", None, "tensor"),
            P("tensor", "dp"),
            P("dp", None, "tensor"),
            P("tensor", "dp"),
        ),
        check_vma=False,
    )
```
